32 devices in a mesh: gx: 4 (over z), gy: 4 (over y, x), gz: 2 (over core).
Axes of the slice: x: 2, y: 2, z: 4, core: 2. Of those that a mesh axis runs over, the one named last changes fastest.
Arguments:
- u_old: float32 [3, 32, 32, 256], P(None, 'gx', 'gy', 'gz'), may hold values from -1.2 to 1.2
- u_trial: float32 [3, 32, 32, 256], P(None, 'gx', 'gy', 'gz'), may hold values from -3.6 to 3.6
- jacobian_inverse: float32 [3, 3, 32, 32, 256], P(None, None, 'gx', 'gy', 'gz'), may hold values from -0.6 to 1.5
- tile_base: int32 [2048], P(('gx', 'gy', 'gz')), may hold values from 0 to 63
- pair_codes: int32 [4, 2048, 128], P(None, ('gx', 'gy', 'gz')), may hold values from 0 to 127, as said below
- pair_groups: int32 [2048, 128], P(('gx', 'gy', 'gz')), may hold values from 0 to 2, as said below
Outputs:
- u_final: float32 [3, 32, 32, 256], P(None, 'gx', 'gy', 'gz')
- residual_norms: float32 [3], replicated
The draws below stay inside these ranges and needn't reach their ends.
Inputs may be any that keep to these rules, and one draw needn't show every extreme that they name: `pair_groups`: on each device the tiles that hold a nonempty slot come first, and their first slot is never empty; every slot of the later tiles is 2. A device holds between 16 and 64 such tiles, and some device holds 64. `pair_codes`: Rows: first node 0 to 127, second direction 0 to 5, third offset 0 to 26, fourth direction 0 to 5; every node of a pair lies in the device's cells extended by one cell on every side.
All inputs are finite; a program needn't handle non-finite values.
Results may differ from the reference program's by a relative error of at most 0.0003.
Values sent between devices are 32-bit elements; how exact they have to be, the bound alone decides.
No kernel may reach another device: no remote copies, remote signals or barrier semaphores. Data moves between devices by JAX's collectives and lax.ppermute only.
A program may use at most 64 MiB of HBM per device.

```python
import jax
import jax.numpy as jnp
from jax import lax

BX = 8
BY = 8
BZ = 128
ITERS = 3
TILES = 64
TILES_ALL = 2048
NX = 32
NY = 32
NZ = 256
N_GX = 4
N_GY = 4
N_GZ = 2


def tile_layout(key):
    keys = jax.random.split(jax.random.fold_in(key, 7), 5)
    blocks_y = BY // 4
    blocks_z = BZ // 8
    tile_anchor = jax.random.randint(keys[0], (TILES_ALL,), 0, BX // 4 * blocks_y * blocks_z)
    inside = jax.random.randint(keys[1], (TILES_ALL, 128), 0, 128)
    along_code = jax.random.randint(keys[2], (TILES_ALL, 128), 0, 6)
    offset = jax.random.randint(keys[3], (TILES_ALL, 128), 0, 27)
    across_code = jax.random.randint(keys[4], (TILES_ALL, 128), 0, 6)
    anchor = tile_anchor[:, None]
    block_x = anchor // (blocks_y * blocks_z)
    block_y = anchor // blocks_z % blocks_y
    block_z = anchor % blocks_z
    third_x = block_x * 4 + inside // 32 + 1 + offset // 9 - 1
    third_y = block_y * 4 + inside // 8 % 4 + 1 + offset // 3 % 3 - 1
    third_z = block_z * 8 + inside % 8 + 1 + offset % 3 - 1
    which_axis = across_code // 2
    negative = across_code % 2 == 1
    coordinate = jnp.where(which_axis == 0, third_x, jnp.where(which_axis == 1, third_y, third_z))
    limit = jnp.where(which_axis == 0, BX + 1, jnp.where(which_axis == 1, BY + 1, BZ + 1))
    fixed_code = jnp.where(negative & (coordinate == 0), across_code - 1, across_code)
    fixed_code = jnp.where(jnp.logical_not(negative) & (coordinate == limit), across_code + 1, fixed_code)
    codes = jnp.stack([inside, along_code, offset, fixed_code]).astype(jnp.int32)
    return (tile_anchor.astype(jnp.int32), codes)


def draw_tile_base(key, part):
    return tile_layout(key)[0]


def draw_pair_codes(key, part):
    return tile_layout(key)[1]


def draw_pair_groups(key, part):
    keys = jax.random.split(jax.random.fold_in(key, 13), 4)
    device_count = TILES_ALL // TILES
    spread = jax.random.randint(keys[0], (device_count,), 0, 1024)
    live_count = TILES // 4 + 3 * TILES // 4 * spread * spread // (1024 * 1024)
    fullest = jax.random.randint(keys[1], (), 0, device_count)
    live_count = jnp.where(jnp.arange(device_count) == fullest, TILES, live_count)
    live_count = jnp.maximum(live_count, 1)
    kinds = jax.random.randint(keys[2], (TILES_ALL, 128), 0, 10)
    groups = jnp.where(kinds < 6, 0, jnp.where(kinds < 9, 1, 2))
    first_kind = jax.random.randint(keys[3], (TILES_ALL,), 0, 2)
    groups = groups.at[:, 0].set(first_kind)
    tile_rank = jnp.arange(TILES_ALL) % TILES
    device_live = jnp.repeat(live_count, TILES, total_repeat_length=TILES_ALL)
    return jnp.where((tile_rank < device_live)[:, None], groups, 2).astype(jnp.int32)


def draw_u_trial(key, part):
    shape = (3, NX, NY, NZ)
    coord_x = lax.broadcasted_iota(jnp.float32, shape, 1) / NX
    coord_y = lax.broadcasted_iota(jnp.float32, shape, 2) / NY
    coord_z = lax.broadcasted_iota(jnp.float32, shape, 3) / NZ
    scale = 1.0 + 2.0 * (coord_x + coord_y + coord_z) / 3.0
    values = 0.3 * jnp.clip(jax.random.normal(key, shape, jnp.float32), -3.0, 3.0) * scale
    return values


def draw_jacobian_inverse(key, part):
    keys = jax.random.split(key, 2)
    shape = (3, 3, NX, NY, NZ)
    diagonal = jnp.exp(jax.random.uniform(keys[0], shape, jnp.float32, jnp.log(0.5), jnp.log(1.5)))
    beside = jnp.clip(0.25 * jax.random.normal(keys[1], shape, jnp.float32), -0.6, 0.6)
    on_diagonal = lax.broadcasted_iota(jnp.int32, shape, 0) == lax.broadcasted_iota(jnp.int32, shape, 1)
    return jnp.where(on_diagonal, diagonal, beside)


def level_of(own_key, extent, cuts, least, largest):
    def one(dim, shards_of):
        steps = jax.random.uniform(jax.random.fold_in(jax.random.fold_in(own_key, 6), dim), (shards_of,), jnp.float32, least / len(cuts), largest / len(cuts))
        return jnp.repeat(jnp.exp(steps), extent[dim] // shards_of).reshape((-1,) + (1,) * (len(extent) - dim - 1))

    level = one(*cuts[0])
    for cut in cuts[1:]:
        level = level * one(*cut)
    return level


def noise(own_key, dims, width, reach, cuts=(), kind=jnp.bfloat16):
    entries = width * jax.random.normal(own_key, dims, jnp.float32)
    if cuts:
        entries = entries * level_of(own_key, dims, cuts, -0.22, 0.18)
    return jnp.clip(entries, -reach, reach).astype(kind)


def setup_inputs(seed: int = 0) -> dict:
    splits = jax.random.split(jax.random.key(seed), 7)
    return {
        "u_old": noise(splits[0], (3, NX, NY, NZ), 0.2, 1.2, ((1, 4), (2, 4), (3, 2)), jnp.float32),
        "u_trial": draw_u_trial(jax.random.fold_in(splits[6], 71), 0),
        "jacobian_inverse": draw_jacobian_inverse(jax.random.fold_in(splits[6], 71), 0),
        "tile_base": draw_tile_base(jax.random.fold_in(splits[6], 71), 0),
        "pair_codes": draw_pair_codes(jax.random.fold_in(splits[6], 71), 0),
        "pair_groups": draw_pair_groups(jax.random.fold_in(splits[6], 71), 0),
    }


step_size = 0.5
stiffness = 0.5
core_square = 0.5

def unit_step(step_code):
    which_axis = step_code // 2
    direction = 1 - 2 * (step_code % 2)
    return [jnp.where(which_axis == k, direction, 0) for k in range(3)]

def pair_cells(tile_anchor, pair_code, blocks_y, blocks_z):
    anchor = tile_anchor[:, None]
    block_x = anchor // (blocks_y * blocks_z)
    block_y = anchor // blocks_z % blocks_y
    block_z = anchor % blocks_z
    inside = pair_code[0]
    first_node = [block_x * 4 + inside // 32 + 1, block_y * 4 + inside // 8 % 4 + 1, block_z * 8 + inside % 8 + 1]
    along_step = unit_step(pair_code[1])
    second_node = [first_node[k] + along_step[k] for k in range(3)]
    offset = pair_code[2]
    third_node = [first_node[0] + offset // 9 - 1, first_node[1] + offset // 3 % 3 - 1, first_node[2] + offset % 3 - 1]
    across_step = unit_step(pair_code[3])
    fourth_node = [third_node[k] + across_step[k] for k in range(3)]
    return [first_node, second_node, third_node, fourth_node]

def pair_terms(flat_u, node_cells, groups, frozen_too, flat_fn):
    points = []
    for node_cell in node_cells:
        lattice = jnp.stack(node_cell).astype(jnp.float32)
        points.append(lattice + flat_u[:, flat_fn(node_cell)])
    line_one = points[1] - points[0]
    line_two = points[3] - points[2]
    separation = 0.5 * (points[2] + points[3]) - 0.5 * (points[0] + points[1])
    square = lax.optimization_barrier(jnp.sum(separation * separation, 0)) + core_square
    coupling = stiffness * lax.optimization_barrier(jnp.sum(line_one * line_two, 0)) / (square * jnp.sqrt(square))
    push_force = coupling * separation
    pieces = [push_force * (groups == 0).astype(jnp.float32)]
    if frozen_too:
        pieces.append(push_force * (groups == 1).astype(jnp.float32))
    halves = 0.5 * jnp.concatenate(pieces, 0)
    return jnp.concatenate([-halves, -halves, halves, halves], 1)

def reference(u_old, u_trial, jacobian_inverse, tile_base, pair_codes, pair_groups):
    device_count = N_GX * N_GY * N_GZ
    blocks_y = BY // 4
    blocks_z = BZ // 8
    width_y = NY + 2
    width_z = NZ + 2
    anchor_dev = tile_base.reshape(device_count, TILES)
    codes_dev = jnp.transpose(pair_codes.reshape(4, device_count, TILES, 128), (1, 0, 2, 3))
    groups_dev = pair_groups.reshape(device_count, TILES, 128)

    def forces(current, frozen_too):
        padded = jnp.pad(current, ((0, 0), (1, 1), (1, 1), (1, 1))).reshape(3, -1)
        channels = 6 if frozen_too else 3

        def one_device(summed, inputs):
            device, tile_anchor, pair_code, groups = inputs
            start_x = device // (N_GY * N_GZ) * BX
            start_y = device // N_GZ % N_GY * BY
            start_z = device % N_GZ * BZ

            def flat_fn(node_cell):
                return ((start_x + node_cell[0]) * width_y + start_y + node_cell[1]) * width_z + start_z + node_cell[2]
            node_cells = pair_cells(tile_anchor, pair_code, blocks_y, blocks_z)
            values = pair_terms(padded, node_cells, groups, frozen_too, flat_fn)
            flat_index = jnp.concatenate([flat_fn(node_cell) for node_cell in node_cells], 0)
            summed = summed.at[:, flat_index.reshape(-1)].add(values.reshape(channels, -1))
            return (summed, None)
        initial = jnp.zeros((channels, padded.shape[1]), jnp.float32)
        summed, _ = lax.scan(one_device, initial, (jnp.arange(device_count, dtype=jnp.int32), anchor_dev, codes_dev, groups_dev))
        return summed.reshape(channels, NX + 2, NY + 2, NZ + 2)[:, 1:-1, 1:-1, 1:-1]
    current = u_trial
    all_forces = forces(current, True)
    frozen = all_forces[3:]
    force_sum = all_forces[:3] + frozen
    norm_list = []
    for iteration in range(ITERS):
        if iteration > 0:
            force_sum = forces(current, False) + frozen
        residual = current - u_old - step_size * force_sum
        norm_list.append(jnp.sqrt(jnp.sum(residual * residual) / (3.0 * NX * NY * NZ)))
        applied = [sum((jacobian_inverse[r, m] * residual[m] for m in range(3))) for r in range(3)]
        current = current - jnp.stack(applied)
    return (current, jnp.stack(norm_list))
```

```python
import functools

import jax
import jax.numpy as jnp
from jax import lax
from jax.experimental import pallas as pl
from jax.experimental.pallas import tpu as pltpu
from jax.sharding import PartitionSpec as P

ITERS = 3
step_size = 0.5
stiffness = 0.5
core_square = 0.5

F32 = jnp.float32
BF16 = jnp.bfloat16
GROUP = 8


class Geo:
    def __init__(self, sx, sy, sz, tiles):
        self.sx, self.sy, self.sz, self.tiles = sx, sy, sz, tiles
        self.X, self.Y = sx + 2, sy + 2
        self.XY = self.X * self.Y
        self.LP = -(-self.XY // 128) * 128
        self.RP = -(-self.XY // 8) * 8
        self.ZR = sz + 8
        self.by = sy // 4
        self.bz = sz // 8
        self.slab = -(-(2 * max(self.X, self.Y) + 2) // 8) * 8


def roll(x, shift, size):
    return pltpu.roll(x, shift % size, 1)


def lane_xy(geo, shape):
    lane = lax.broadcasted_iota(jnp.int32, shape, len(shape) - 1)
    x = jnp.zeros_like(lane)
    for k in range(1, geo.X):
        x = x + (lane >= k * geo.Y).astype(jnp.int32)
    return lane, x, lane - x * geo.Y


def add_rows_x(geo, rows, low, high, has_low, has_high):
    lane, _, _ = lane_xy(geo, rows.shape)
    span = geo.sx * geo.Y
    from_low = roll(low, -span, geo.LP)
    from_high = roll(high, span, geo.LP)
    rows = rows + jnp.where((lane < 2 * geo.Y) & has_low, from_low, 0.0)
    return rows + jnp.where((lane >= span) & (lane < geo.XY) & has_high, from_high, 0.0)


def add_rows_y(geo, rows, low, high, has_low, has_high):
    lane, _, y = lane_xy(geo, rows.shape)
    from_low = roll(low, -geo.sy, geo.LP)
    from_high = roll(high, geo.sy, geo.LP)
    inside = lane < geo.XY
    rows = rows + jnp.where((y < 2) & inside & has_low, from_low, 0.0)
    return rows + jnp.where((y >= geo.sy) & inside & has_high, from_high, 0.0)


def fill_z_kernel(geo, ut, uo, ji, face, zbuf, wide):
    wide[...] = jnp.zeros_like(wide)
    zbuf[...] = jnp.zeros_like(zbuf)
    sources = [ut.at[c] for c in range(3)] + [uo.at[c] for c in range(3)] + [ji.at[c] for c in range(9)]
    for c, source in enumerate(sources):
        for x in range(geo.sx):
            start = (x + 1) * geo.Y + 1
            wide[start : start + geo.sy, :] = source[x * geo.sy : (x + 1) * geo.sy, :]
        value = wide[...]
        face[c] = value[: geo.RP]
        turned = value.T
        zbuf[c : c + 1, :] = turned[0:1]
        zbuf[16 + c : 17 + c, :] = turned[geo.sz - 1 : geo.sz]


def fill_rows(flags, z_low, z_high):
    low = jnp.where(flags[4] > 0, z_low[16:32, :], 0.0)
    high = jnp.where(flags[5] > 0, z_high[0:16, :], 0.0)
    return jnp.concatenate([low, high], 0)


def fill_x_kernel(geo, flags, ut, uo, ji, z_low, z_high, x_low, x_high):
    rows = fill_rows(flags, z_low, z_high)
    count = 15 * geo.sy
    sources = [ut.at[c] for c in range(3)] + [uo.at[c] for c in range(3)] + [ji.at[c] for c in range(9)]
    last = (geo.sx - 1) * geo.sy
    for c, source in enumerate(sources):
        x_low[c * geo.sy : (c + 1) * geo.sy, :] = source[0 : geo.sy, :]
        x_high[c * geo.sy : (c + 1) * geo.sy, :] = source[last : last + geo.sy, :]
    x_low[count : count + 32, :] = rows
    x_high[count : count + 32, :] = rows


def fill_y_kernel(geo, flags, face, z_low, z_high, from_low, from_high, out, rows_out, y_low, y_high):
    has_low, has_high = flags[0] > 0, flags[1] > 0
    count = 15 * geo.sy
    rows = add_rows_x(
        geo,
        fill_rows(flags, z_low, z_high),
        from_low[count : count + 32, :],
        from_high[count : count + 32, :],
        has_low,
        has_high,
    )
    rows_out[...] = rows
    out[...] = face[...]
    y_low[...] = jnp.zeros_like(y_low)
    y_high[...] = jnp.zeros_like(y_high)
    top = (geo.sx + 1) * geo.Y + 1
    for c in range(15):
        part = slice(c * geo.sy, (c + 1) * geo.sy)
        out[c, 1 : 1 + geo.sy, :] = jnp.where(has_low, from_low[part, :], 0.0)
        out[c, top : top + geo.sy, :] = jnp.where(has_high, from_high[part, :], 0.0)
        into = slice(c * geo.X, (c + 1) * geo.X)
        y_low[into, :] = out[c, pl.ds(1, geo.X, stride=geo.Y), :]
        y_high[into, :] = out[c, pl.ds(geo.sy, geo.X, stride=geo.Y), :]
    tail = fill_y_rows(geo) - 32
    y_low[tail : tail + 32, :] = rows
    y_high[tail : tail + 32, :] = rows


def fill_y_rows(geo):
    return -(-15 * geo.X // 8) * 8 + 32


def fill_done(geo, flags, face, rows_in, from_low, from_high, wide, targets):
    has_low, has_high = flags[2] > 0, flags[3] > 0
    tail = fill_y_rows(geo) - 32
    rows = add_rows_y(
        geo,
        rows_in[...],
        from_low[tail : tail + 32, :],
        from_high[tail : tail + 32, :],
        has_low,
        has_high,
    )
    wide[...] = jnp.zeros_like(wide)
    for c, target in enumerate(targets):
        wide[: geo.RP, :] = face[c]
        part = slice(c * geo.X, (c + 1) * geo.X)
        wide[pl.ds(0, geo.X, stride=geo.Y), :] = jnp.where(has_low, from_low[part, :], 0.0)
        wide[pl.ds(geo.sy + 1, geo.X, stride=geo.Y), :] = jnp.where(has_high, from_high[part, :], 0.0)
        target[0:8, :] = jnp.zeros((8, geo.LP), F32)
        target[geo.ZR - 8 : geo.ZR, :] = jnp.zeros((8, geo.LP), F32)
        target[2 : 2 + geo.sz, :] = wide[...].T
        target[1:2, :] = rows[c : c + 1]
        target[geo.sz + 2 : geo.sz + 3, :] = rows[16 + c : 17 + c]


def z_slab(geo, force, zbuf):
    zbuf[...] = jnp.zeros_like(zbuf)
    for c in range(3):
        zbuf[c, 0:2, :] = force[c, 1:3, :]
        zbuf[c, 2:4, :] = force[c, geo.sz + 1 : geo.sz + 3, :]


def sum_x_kernel(geo, flags, force, z_low, z_high, face, rows_out, x_low, x_high):
    has_low, has_high = flags[4] > 0, flags[5] > 0
    rows_out[...] = jnp.zeros_like(rows_out)
    x_low[...] = jnp.zeros_like(x_low)
    x_high[...] = jnp.zeros_like(x_high)
    span, two = geo.sx * geo.Y, 2 * geo.Y
    row = lax.broadcasted_iota(jnp.int32, (geo.sz, geo.LP), 0)
    for c in range(3):
        low = jnp.where(has_low, z_low[c, 2:4, :], 0.0)
        high = jnp.where(has_high, z_high[c, 0:2, :], 0.0)
        value = force[c, 2 : 2 + geo.sz, :]
        value = value + jnp.where(row == 0, low[1:2], 0.0)
        value = value + jnp.where(row == geo.sz - 1, high[0:1], 0.0)
        turned = value.T[: geo.RP]
        face[c] = turned
        low_row = force[c, 1:2, :] + low[0:1]
        high_row = force[c, geo.sz + 2 : geo.sz + 3, :] + high[1:2]
        rows_out[c : c + 1, :] = low_row
        rows_out[4 + c : 5 + c, :] = high_row
        x_low[c, 0:two, :] = face[c, 0:two, :]
        x_high[c, 0:two, :] = face[c, span : span + two, :]
        for buffer in (x_low, x_high):
            buffer[c, two : two + 1, :] = low_row
            buffer[c, two + 1 : two + 2, :] = high_row


def slab_rows(buffer, at):
    zero = jnp.zeros_like(buffer[0, at : at + 1, :])
    low = [buffer[c, at : at + 1, :] for c in range(3)]
    high = [buffer[c, at + 1 : at + 2, :] for c in range(3)]
    return jnp.concatenate(low + [zero] + high + [zero], 0)


def sum_y_kernel(geo, flags, face, rows_in, from_low, from_high, out, rows_out, y_low, y_high):
    has_low, has_high = flags[0] > 0, flags[1] > 0
    span, two = geo.sx * geo.Y, 2 * geo.Y
    rows = add_rows_x(
        geo, rows_in[...], slab_rows(from_low, two), slab_rows(from_high, two), has_low, has_high
    )
    rows_out[...] = rows
    out[...] = face[...]
    y_low[...] = jnp.zeros_like(y_low)
    y_high[...] = jnp.zeros_like(y_high)
    for c in range(3):
        out[c, 0:two, :] += jnp.where(has_low, from_low[c, 0:two, :], 0.0)
        out[c, span : span + two, :] += jnp.where(has_high, from_high[c, 0:two, :], 0.0)
        for plane in range(2):
            into = slice(plane * geo.X, (plane + 1) * geo.X)
            y_low[c, into, :] = out[c, pl.ds(plane, geo.X, stride=geo.Y), :]
            y_high[c, into, :] = out[c, pl.ds(geo.sy + plane, geo.X, stride=geo.Y), :]
        at = 2 * geo.X
        for buffer in (y_low, y_high):
            buffer[c, at : at + 1, :] = rows[c : c + 1]
            buffer[c, at + 1 : at + 2, :] = rows[4 + c : 5 + c]


def sum_done(geo, flags, face, rows_in, from_low, from_high, wide, total):
    has_low, has_high = flags[2] > 0, flags[3] > 0
    at = 2 * geo.X
    rows = add_rows_y(
        geo, rows_in[...], slab_rows(from_low, at), slab_rows(from_high, at), has_low, has_high
    )
    wide[...] = jnp.zeros_like(wide)
    for c in range(3):
        wide[: geo.RP, :] = face[c]
        for plane in range(2):
            part = slice(plane * geo.X, (plane + 1) * geo.X)
            low_at = pl.ds(plane, geo.X, stride=geo.Y)
            high_at = pl.ds(geo.sy + plane, geo.X, stride=geo.Y)
            wide[low_at, :] = wide[low_at, :] + jnp.where(has_low, from_low[c, part, :], 0.0)
            wide[high_at, :] = wide[high_at, :] + jnp.where(has_high, from_high[c, part, :], 0.0)
        total[c, 0:8, :] = jnp.zeros((8, geo.LP), F32)
        total[c, geo.ZR - 8 : geo.ZR, :] = jnp.zeros((8, geo.LP), F32)
        total[c, 2 : 2 + geo.sz, :] = wide[...].T
        total[c, 1:2, :] = rows[c : c + 1]
        total[c, geo.sz + 2 : geo.sz + 3, :] = rows[4 + c : 5 + c]


def update(geo, total, u, u_old, jinv, new_u, norm):
    lane, x, y = lane_xy(geo, (8, geo.LP))
    owned = (x >= 1) & (x <= geo.sx) & (y >= 1) & (y <= geo.sy)
    squares = jnp.zeros((8, geo.LP), F32)
    for k in range(geo.ZR // 8):
        rows = slice(8 * k, 8 * k + 8)
        now = [u[c, rows, :] for c in range(3)]
        residual = [now[c] - u_old[c, rows, :] - step_size * total[c, rows, :] for c in range(3)]
        for r in range(3):
            applied = sum(jinv[3 * r + m, rows, :] * residual[m] for m in range(3))
            new_u[r, rows, :] = now[r] - applied
        z = lax.broadcasted_iota(jnp.int32, (8, geo.LP), 0) + (8 * k - 1)
        mask = owned & (z >= 1) & (z <= geo.sz)
        square = residual[0] * residual[0] + residual[1] * residual[1] + residual[2] * residual[2]
        squares = squares + jnp.where(mask, square, 0.0)
    norm[...] = squares


def steps(code):
    which = code >> 1
    direction = 1 - 2 * (code & 1)
    return [jnp.where(which == k, direction, 0) for k in range(3)]


def split(value):
    high = value.astype(BF16).astype(F32)
    return high, value - high


def pair_pass(geo, base, u, codes, groups, both, work, frozen, force):
    windows, hots, gathered, sums = work
    LP, Y = geo.LP, geo.Y
    for k in range(geo.bz):
        window = u[:, 8 * k : 8 * k + 16, :].reshape(48, LP)
        high = window.astype(BF16)
        windows[k, :, :LP] = high
        windows[k, :, LP:] = (window - high.astype(F32)).astype(BF16)
    sums[...] = jnp.zeros_like(sums)
    lanes = lax.broadcasted_iota(jnp.int32, (LP, 512), 0)
    depths = lax.broadcasted_iota(jnp.int32, (16, 512), 0)

    def one_group(turn, carry):
        rows = pl.ds(pl.multiple_of(turn * GROUP, GROUP), GROUP)
        inside, along, offset, across = [codes[k, rows, :] for k in range(4)]
        kind = groups[rows, :]
        e1, e3 = steps(along), steps(across)
        third = (offset * 43) >> 7
        ninth = (offset * 57) >> 9
        shift = [ninth - 1, third - 3 * ninth - 1, offset - 3 * third - 1]
        lane_a = ((inside >> 5) + 1) * Y + ((inside >> 3) & 3) + 1
        depth_a = (inside & 7) + 2
        lane_b = lane_a + e1[0] * Y + e1[1]
        depth_b = depth_a + e1[2]
        lane_c = lane_a + shift[0] * Y + shift[1]
        depth_c = depth_a + shift[2]
        lane_d = lane_c + e3[0] * Y + e3[1]
        depth_d = depth_c + e3[2]
        lane4 = jnp.concatenate([lane_a, lane_b, lane_c, lane_d], 1)
        depth4 = jnp.concatenate([depth_a, depth_b, depth_c, depth_d], 1)
        places = []
        for t in range(GROUP):
            anchor = base[turn * GROUP + t]
            place = lax.rem(anchor, geo.bz)
            plane = lax.div(anchor, geo.bz)
            corner = 4 * Y * lax.div(plane, geo.by) + 4 * lax.rem(plane, geo.by)
            places.append(place)
            hot = jnp.where(lanes == lane4[t : t + 1] + corner, 1.0, 0.0).astype(BF16)
            hots[t] = hot
            picked = jnp.dot(
                windows[place], jnp.concatenate([hot, hot], 0), preferred_element_type=F32
            )
            mask = depths == depth4[t : t + 1]
            for c in range(3):
                part = jnp.where(mask, picked[16 * c : 16 * c + 16], 0.0)
                gathered[c, t : t + 1, :] = jnp.sum(part, 0, keepdims=True)
        line_one, line_two, apart = [], [], []
        for c in range(3):
            ua, ub, uc, ud = [gathered[c, :, 128 * n : 128 * n + 128] for n in range(4)]
            step1, step3 = e1[c].astype(F32), e3[c].astype(F32)
            line_one.append((ub - ua) + step1)
            line_two.append((ud - uc) + step3)
            lattice = shift[c].astype(F32) + 0.5 * (step3 - step1)
            apart.append(0.5 * ((uc + ud) - (ua + ub)) + lattice)
        square = apart[0] * apart[0] + apart[1] * apart[1] + apart[2] * apart[2] + core_square
        product = (
            line_one[0] * line_two[0] + line_one[1] * line_two[1] + line_one[2] * line_two[2]
        )
        coupling = (0.5 * stiffness) * product / (square * jnp.sqrt(square))
        pieces = []
        for group in (0, 1) if both else (0,):
            chosen = jnp.where(kind == group, coupling, 0.0)
            halves = [split(chosen * apart[c]) for c in range(3)]
            for piece in range(2):
                for c in range(3):
                    h = halves[c][piece]
                    pieces.append(jnp.concatenate([-h, -h, h, h], 1))
        for t in range(GROUP):
            mask = depths == depth4[t : t + 1]
            spread = jnp.concatenate(
                [jnp.where(mask, piece[t : t + 1], 0.0) for piece in pieces], 0
            ).astype(BF16)
            pushed = lax.dot_general(
                spread, hots[t], (((1,), (1,)), ((), ())), preferred_element_type=F32
            )
            for group in range(2 if both else 1):
                part = pushed[96 * group : 96 * group + 48] + pushed[96 * group + 48 : 96 * group + 96]
                sums[group, places[t]] += part
        return carry

    lax.fori_loop(0, geo.tiles // GROUP, one_group, 0)

    def folded(group, c, k):
        rows = jnp.zeros((8, LP), F32)
        if k < geo.bz:
            rows = rows + sums[group, k, 16 * c : 16 * c + 8, :]
        if k > 0:
            rows = rows + sums[group, k - 1, 16 * c + 8 : 16 * c + 16, :]
        return rows

    for c in range(3):
        for k in range(geo.bz + 1):
            rows = slice(8 * k, 8 * k + 8)
            if both:
                frozen[c, rows, :] = folded(1, c, k)
            force[c, rows, :] = folded(0, c, k) + frozen[c, rows, :]


def first_kernel(
    geo, base, flags, face, rows_in, from_low, from_high, codes, groups,
    u, u_old, jinv, frozen, force, zbuf, wide, *work,
):
    targets = [u.at[c] for c in range(3)] + [u_old.at[c] for c in range(3)]
    targets = targets + [jinv.at[c] for c in range(9)]
    fill_done(geo, flags, face, rows_in, from_low, from_high, wide, targets)
    pair_pass(geo, base, u, codes, groups, True, work, frozen, force)
    z_slab(geo, force, zbuf)


def next_kernel(
    geo, base, flags, face, rows_in, from_low, from_high, u, u_old, jinv, frozen, codes, groups,
    new_u, norm, force, zbuf, wide, total, *work,
):
    sum_done(geo, flags, face, rows_in, from_low, from_high, wide, total)
    update(geo, total, u, u_old, jinv, new_u, norm)
    pair_pass(geo, base, new_u, codes, groups, False, work, frozen, force)
    z_slab(geo, force, zbuf)


def last_kernel(
    geo, flags, face, rows_in, from_low, from_high, u, u_old, jinv, norm_0, norm_1,
    out, norms, wide, total, new_u, norm_2,
):
    sum_done(geo, flags, face, rows_in, from_low, from_high, wide, total)
    update(geo, total, u, u_old, jinv, new_u, norm_2)
    for c in range(3):
        wide[...] = new_u[c, 2 : 2 + geo.sz, :].T
        for x in range(geo.sx):
            start = (x + 1) * geo.Y + 1
            out[c, x * geo.sy : (x + 1) * geo.sy, :] = wide[start : start + geo.sy, :]
    lane = lax.broadcasted_iota(jnp.int32, (1, geo.LP), 1)
    line = jnp.zeros((1, geo.LP), F32)
    for k, norm in enumerate((norm_0, norm_1, norm_2)):
        line = line + jnp.where(lane == k, jnp.sum(norm[...]), 0.0)
    norms[...] = jnp.broadcast_to(line, norms.shape)


def ring(shard, axis, by):
    count = lax.axis_size(axis)
    return lax.ppermute(shard, axis, [(i, (i + by) % count) for i in range(count)])


def swap(low_buffer, high_buffer, axis):
    return ring(high_buffer, axis, 1), ring(low_buffer, axis, -1)


def swap_joint(buffer, axis):
    if lax.axis_size(axis) <= 2:
        other = ring(buffer, axis, 1)
        return other, other
    return ring(buffer, axis, 1), ring(buffer, axis, -1)


def per_device(u_old, u_trial, jacobian_inverse, tile_base, pair_codes, pair_groups):
    sx, sy, sz = u_old.shape[1:]
    geo = Geo(sx, sy, sz, tile_base.shape[0])
    if sz != 128 or geo.LP != 128 or sy % 8 or geo.tiles % GROUP:
        raise ValueError("unsupported sizes")
    axes = ("gx", "gy", "gz")
    cells = 3.0 * sx * sy * sz
    devices = 1
    limits = []
    for axis in axes:
        cells = cells * lax.axis_size(axis)
        devices = devices * lax.axis_size(axis)
        at = lax.axis_index(axis)
        limits += [(at > 0).astype(jnp.int32), (at < lax.axis_size(axis) - 1).astype(jnp.int32)]
    flags = jnp.stack(limits)
    vmem, smem = pl.BlockSpec(memory_space=pltpu.VMEM), pl.BlockSpec(memory_space=pltpu.SMEM)

    def arr(*shape):
        return jax.ShapeDtypeStruct(shape, F32)

    def call(kernel, name, scalars, operands, outs, scratch=()):
        return pl.pallas_call(
            functools.partial(kernel, geo),
            out_shape=outs,
            in_specs=[smem] * len(scalars) + [vmem] * len(operands),
            out_specs=[vmem] * len(outs),
            scratch_shapes=list(scratch),
            name=name,
        )(*scalars, *operands)

    def spot(*shape, dtype=F32):
        return pltpu.VMEM(shape, dtype)

    def work(count):
        return [
            spot(geo.bz, 48, 2 * geo.LP, dtype=BF16),
            spot(GROUP, geo.LP, 512, dtype=BF16),
            spot(3, GROUP, 512),
            spot(count, geo.bz, 48, geo.LP),
        ]

    square = spot(geo.LP, sz)
    lattice = arr(3, geo.ZR, geo.LP)
    faces3, rows8, zshape = arr(3, geo.RP, sz), arr(8, geo.LP), arr(3, 8, geo.LP)
    slab = arr(3, geo.slab, 128)

    ut = u_trial.reshape(3, sx * sy, sz)
    uo = u_old.reshape(3, sx * sy, sz)
    ji = jacobian_inverse.reshape(9, sx * sy, sz)

    face, zbuf = call(
        fill_z_kernel, "fill_z", [], [ut, uo, ji], [arr(15, geo.RP, sz), arr(32, geo.LP)], [square]
    )
    z_low, z_high = swap_joint(zbuf, "gz")
    wide_x = arr(15 * sy + 32, 128)
    x_low, x_high = call(
        fill_x_kernel, "fill_x", [flags], [ut, uo, ji, z_low, z_high], [wide_x, wide_x]
    )
    from_low, from_high = swap(x_low, x_high, "gx")
    wide_y = arr(fill_y_rows(geo), 128)
    face, rows, y_low, y_high = call(
        fill_y_kernel,
        "fill_y",
        [flags],
        [face, z_low, z_high, from_low, from_high],
        [arr(15, geo.RP, sz), arr(32, geo.LP), wide_y, wide_y],
    )
    from_low, from_high = swap(y_low, y_high, "gy")
    u, uo_l, ji_l, frozen, force, zbuf = call(
        first_kernel,
        "first_pass",
        [tile_base, flags],
        [face, rows, from_low, from_high, pair_codes, pair_groups],
        [lattice, lattice, arr(9, geo.ZR, geo.LP), lattice, lattice, zshape],
        [square] + work(2),
    )

    norm_list = []
    for iteration in range(ITERS):
        z_low, z_high = swap_joint(zbuf, "gz")
        face, rows, x_low, x_high = call(
            sum_x_kernel, "sum_x", [flags], [force, z_low, z_high], [faces3, rows8, slab, slab]
        )
        from_low, from_high = swap(x_low, x_high, "gx")
        face, rows, y_low, y_high = call(
            sum_y_kernel,
            "sum_y",
            [flags],
            [face, rows, from_low, from_high],
            [faces3, rows8, slab, slab],
        )
        from_low, from_high = swap(y_low, y_high, "gy")
        total = spot(3, geo.ZR, geo.LP)
        if iteration < ITERS - 1:
            u, norm, force, zbuf = call(
                next_kernel,
                "next_pass",
                [tile_base, flags],
                [face, rows, from_low, from_high, u, uo_l, ji_l, frozen, pair_codes, pair_groups],
                [lattice, rows8, lattice, zshape],
                [square, total] + work(1),
            )
            norm_list.append(norm)
    out, norms = call(
        last_kernel,
        "last",
        [flags],
        [face, rows, from_low, from_high, u, uo_l, ji_l] + norm_list,
        [arr(3, sx * sy, sz), arr(devices, 128)],
        [square, spot(3, geo.ZR, geo.LP), spot(3, geo.ZR, geo.LP), spot(8, geo.LP)],
    )
    spread = lax.all_to_all(norms.reshape(devices, 1, 128), axes, 0, 0)
    squares = jnp.sum(spread, axis=(0, 1))[:ITERS]
    return out.reshape(3, sx, sy, sz), jnp.sqrt(squares / cells)


def solution(mesh):
    return jax.shard_map(
        per_device,
        mesh=mesh,
        in_specs=(
            P(None, "gx", "gy", "gz"),
            P(None, "gx", "gy", "gz"),
            P(None, None, "gx", "gy", "gz"),
            P(("gx", "gy", "gz")),
            P(None, ("gx", "gy", "gz"), None),
            P(("gx", "gy", "gz"), None),
        ),
        out_specs=(P(None, "gx", "gy", "gz"), P()),
        check_vma=False,
    )
```

```python
import functools

import jax
import jax.numpy as jnp
from jax import lax
from jax.experimental import pallas as pl
from jax.experimental.pallas import tpu as pltpu
from jax.sharding import PartitionSpec as P

ITERS = 3
step_size = 0.5
stiffness = 0.5
core_square = 0.5

F32 = jnp.float32
BF16 = jnp.bfloat16
GROUP = 8
VMEM_GRANT = 12 << 20


class Geo:
    def __init__(self, sx, sy, sz, tiles):
        self.sx, self.sy, self.sz, self.tiles = sx, sy, sz, tiles
        self.X, self.Y = sx + 2, sy + 2
        self.XY = self.X * self.Y
        self.LP = -(-self.XY // 128) * 128
        self.RP = -(-self.XY // 8) * 8
        self.ZR = sz + 8
        self.by = sy // 4
        self.bz = sz // 8
        self.slab = -(-(2 * max(self.X, self.Y) + 2) // 8) * 8


def roll(x, shift, size):
    return pltpu.roll(x, shift % size, 1)


def lane_xy(geo, shape):
    lane = lax.broadcasted_iota(jnp.int32, shape, len(shape) - 1)
    x = jnp.zeros_like(lane)
    for k in range(1, geo.X):
        x = x + (lane >= k * geo.Y).astype(jnp.int32)
    return lane, x, lane - x * geo.Y


def add_rows_x(geo, rows, low, high, has_low, has_high):
    lane, _, _ = lane_xy(geo, rows.shape)
    span = geo.sx * geo.Y
    from_low = roll(low, -span, geo.LP)
    from_high = roll(high, span, geo.LP)
    rows = rows + jnp.where((lane < 2 * geo.Y) & has_low, from_low, 0.0)
    return rows + jnp.where((lane >= span) & (lane < geo.XY) & has_high, from_high, 0.0)


def add_rows_y(geo, rows, low, high, has_low, has_high):
    lane, _, y = lane_xy(geo, rows.shape)
    from_low = roll(low, -geo.sy, geo.LP)
    from_high = roll(high, geo.sy, geo.LP)
    inside = lane < geo.XY
    rows = rows + jnp.where((y < 2) & inside & has_low, from_low, 0.0)
    return rows + jnp.where((y >= geo.sy) & inside & has_high, from_high, 0.0)


def fill_z_kernel(geo, ut, uo, ji, face, zbuf, wide):
    wide[...] = jnp.zeros_like(wide)
    zbuf[...] = jnp.zeros_like(zbuf)
    sources = [ut.at[c] for c in range(3)] + [uo.at[c] for c in range(3)] + [ji.at[c] for c in range(9)]
    for c, source in enumerate(sources):
        for x in range(geo.sx):
            start = (x + 1) * geo.Y + 1
            wide[start : start + geo.sy, :] = source[x * geo.sy : (x + 1) * geo.sy, :]
        value = wide[...]
        face[c] = value[: geo.RP]
        turned = value.T
        zbuf[c : c + 1, :] = turned[0:1]
        zbuf[16 + c : 17 + c, :] = turned[geo.sz - 1 : geo.sz]


def fill_rows(flags, z_low, z_high):
    low = jnp.where(flags[4] > 0, z_low[16:32, :], 0.0)
    high = jnp.where(flags[5] > 0, z_high[0:16, :], 0.0)
    return jnp.concatenate([low, high], 0)


def fill_x_kernel(geo, flags, ut, uo, ji, z_low, z_high, x_low, x_high):
    rows = fill_rows(flags, z_low, z_high)
    count = 15 * geo.sy
    sources = [ut.at[c] for c in range(3)] + [uo.at[c] for c in range(3)] + [ji.at[c] for c in range(9)]
    last = (geo.sx - 1) * geo.sy
    for c, source in enumerate(sources):
        x_low[c * geo.sy : (c + 1) * geo.sy, :] = source[0 : geo.sy, :]
        x_high[c * geo.sy : (c + 1) * geo.sy, :] = source[last : last + geo.sy, :]
    x_low[count : count + 32, :] = rows
    x_high[count : count + 32, :] = rows


def fill_y_kernel(geo, flags, face, z_low, z_high, from_low, from_high, out, rows_out, y_low, y_high):
    has_low, has_high = flags[0] > 0, flags[1] > 0
    count = 15 * geo.sy
    rows = add_rows_x(
        geo,
        fill_rows(flags, z_low, z_high),
        from_low[count : count + 32, :],
        from_high[count : count + 32, :],
        has_low,
        has_high,
    )
    rows_out[...] = rows
    out[...] = face[...]
    y_low[...] = jnp.zeros_like(y_low)
    y_high[...] = jnp.zeros_like(y_high)
    top = (geo.sx + 1) * geo.Y + 1
    for c in range(15):
        part = slice(c * geo.sy, (c + 1) * geo.sy)
        out[c, 1 : 1 + geo.sy, :] = jnp.where(has_low, from_low[part, :], 0.0)
        out[c, top : top + geo.sy, :] = jnp.where(has_high, from_high[part, :], 0.0)
        into = slice(c * geo.X, (c + 1) * geo.X)
        y_low[into, :] = out[c, pl.ds(1, geo.X, stride=geo.Y), :]
        y_high[into, :] = out[c, pl.ds(geo.sy, geo.X, stride=geo.Y), :]
    tail = fill_y_rows(geo) - 32
    y_low[tail : tail + 32, :] = rows
    y_high[tail : tail + 32, :] = rows


def fill_y_rows(geo):
    return -(-15 * geo.X // 8) * 8 + 32


def fill_done(geo, flags, face, rows_in, from_low, from_high, wide, targets):
    has_low, has_high = flags[2] > 0, flags[3] > 0
    tail = fill_y_rows(geo) - 32
    rows = add_rows_y(
        geo,
        rows_in[...],
        from_low[tail : tail + 32, :],
        from_high[tail : tail + 32, :],
        has_low,
        has_high,
    )
    wide[...] = jnp.zeros_like(wide)
    for c, target in enumerate(targets):
        wide[: geo.RP, :] = face[c]
        part = slice(c * geo.X, (c + 1) * geo.X)
        wide[pl.ds(0, geo.X, stride=geo.Y), :] = jnp.where(has_low, from_low[part, :], 0.0)
        wide[pl.ds(geo.sy + 1, geo.X, stride=geo.Y), :] = jnp.where(has_high, from_high[part, :], 0.0)
        target[0:8, :] = jnp.zeros((8, geo.LP), F32)
        target[geo.ZR - 8 : geo.ZR, :] = jnp.zeros((8, geo.LP), F32)
        target[2 : 2 + geo.sz, :] = wide[...].T
        target[1:2, :] = rows[c : c + 1]
        target[geo.sz + 2 : geo.sz + 3, :] = rows[16 + c : 17 + c]


def z_slab(geo, force, zbuf):
    zbuf[...] = jnp.zeros_like(zbuf)
    for c in range(3):
        zbuf[c, 0:2, :] = force[c, 1:3, :]
        zbuf[c, 2:4, :] = force[c, geo.sz + 1 : geo.sz + 3, :]


def sum_x_kernel(geo, flags, force, z_low, z_high, face, rows_out, x_low, x_high):
    has_low, has_high = flags[4] > 0, flags[5] > 0
    rows_out[...] = jnp.zeros_like(rows_out)
    x_low[...] = jnp.zeros_like(x_low)
    x_high[...] = jnp.zeros_like(x_high)
    span, two = geo.sx * geo.Y, 2 * geo.Y
    row = lax.broadcasted_iota(jnp.int32, (geo.sz, geo.LP), 0)
    for c in range(3):
        low = jnp.where(has_low, z_low[c, 2:4, :], 0.0)
        high = jnp.where(has_high, z_high[c, 0:2, :], 0.0)
        value = force[c, 2 : 2 + geo.sz, :]
        value = value + jnp.where(row == 0, low[1:2], 0.0)
        value = value + jnp.where(row == geo.sz - 1, high[0:1], 0.0)
        turned = value.T[: geo.RP]
        face[c] = turned
        low_row = force[c, 1:2, :] + low[0:1]
        high_row = force[c, geo.sz + 2 : geo.sz + 3, :] + high[1:2]
        rows_out[c : c + 1, :] = low_row
        rows_out[4 + c : 5 + c, :] = high_row
        x_low[c, 0:two, :] = face[c, 0:two, :]
        x_high[c, 0:two, :] = face[c, span : span + two, :]
        for buffer in (x_low, x_high):
            buffer[c, two : two + 1, :] = low_row
            buffer[c, two + 1 : two + 2, :] = high_row


def slab_rows(buffer, at):
    zero = jnp.zeros_like(buffer[0, at : at + 1, :])
    low = [buffer[c, at : at + 1, :] for c in range(3)]
    high = [buffer[c, at + 1 : at + 2, :] for c in range(3)]
    return jnp.concatenate(low + [zero] + high + [zero], 0)


def sum_y_kernel(geo, flags, face, rows_in, from_low, from_high, out, rows_out, y_low, y_high):
    has_low, has_high = flags[0] > 0, flags[1] > 0
    span, two = geo.sx * geo.Y, 2 * geo.Y
    rows = add_rows_x(
        geo, rows_in[...], slab_rows(from_low, two), slab_rows(from_high, two), has_low, has_high
    )
    rows_out[...] = rows
    out[...] = face[...]
    y_low[...] = jnp.zeros_like(y_low)
    y_high[...] = jnp.zeros_like(y_high)
    for c in range(3):
        out[c, 0:two, :] += jnp.where(has_low, from_low[c, 0:two, :], 0.0)
        out[c, span : span + two, :] += jnp.where(has_high, from_high[c, 0:two, :], 0.0)
        for plane in range(2):
            into = slice(plane * geo.X, (plane + 1) * geo.X)
            y_low[c, into, :] = out[c, pl.ds(plane, geo.X, stride=geo.Y), :]
            y_high[c, into, :] = out[c, pl.ds(geo.sy + plane, geo.X, stride=geo.Y), :]
        at = 2 * geo.X
        for buffer in (y_low, y_high):
            buffer[c, at : at + 1, :] = rows[c : c + 1]
            buffer[c, at + 1 : at + 2, :] = rows[4 + c : 5 + c]


def sum_done(geo, flags, face, rows_in, from_low, from_high, wide, total):
    has_low, has_high = flags[2] > 0, flags[3] > 0
    at = 2 * geo.X
    rows = add_rows_y(
        geo, rows_in[...], slab_rows(from_low, at), slab_rows(from_high, at), has_low, has_high
    )
    wide[...] = jnp.zeros_like(wide)
    for c in range(3):
        wide[: geo.RP, :] = face[c]
        for plane in range(2):
            part = slice(plane * geo.X, (plane + 1) * geo.X)
            low_at = pl.ds(plane, geo.X, stride=geo.Y)
            high_at = pl.ds(geo.sy + plane, geo.X, stride=geo.Y)
            wide[low_at, :] = wide[low_at, :] + jnp.where(has_low, from_low[c, part, :], 0.0)
            wide[high_at, :] = wide[high_at, :] + jnp.where(has_high, from_high[c, part, :], 0.0)
        total[c, 0:8, :] = jnp.zeros((8, geo.LP), F32)
        total[c, geo.ZR - 8 : geo.ZR, :] = jnp.zeros((8, geo.LP), F32)
        total[c, 2 : 2 + geo.sz, :] = wide[...].T
        total[c, 1:2, :] = rows[c : c + 1]
        total[c, geo.sz + 2 : geo.sz + 3, :] = rows[4 + c : 5 + c]


def update(geo, total, u, u_old, jinv, new_u, norm):
    lane, x, y = lane_xy(geo, (8, geo.LP))
    owned = (x >= 1) & (x <= geo.sx) & (y >= 1) & (y <= geo.sy)
    squares = jnp.zeros((8, geo.LP), F32)
    for k in range(geo.ZR // 8):
        rows = slice(8 * k, 8 * k + 8)
        now = [u[c, rows, :] for c in range(3)]
        residual = [now[c] - u_old[c, rows, :] - step_size * total[c, rows, :] for c in range(3)]
        for r in range(3):
            applied = sum(jinv[3 * r + m, rows, :] * residual[m] for m in range(3))
            new_u[r, rows, :] = now[r] - applied
        z = lax.broadcasted_iota(jnp.int32, (8, geo.LP), 0) + (8 * k - 1)
        mask = owned & (z >= 1) & (z <= geo.sz)
        square = residual[0] * residual[0] + residual[1] * residual[1] + residual[2] * residual[2]
        squares = squares + jnp.where(mask, square, 0.0)
    norm[...] = squares


def steps(code):
    which = code >> 1
    direction = 1 - 2 * (code & 1)
    return [jnp.where(which == k, direction, 0) for k in range(3)]


def split(value):
    high = value.astype(BF16).astype(F32)
    return high, value - high


def pair_pass(geo, base, u, codes, groups, both, work, frozen, force):
    windows, hots, gathered, sums = work
    LP, Y = geo.LP, geo.Y
    for k in range(geo.bz):
        window = u[:, 8 * k : 8 * k + 16, :].reshape(48, LP)
        high = window.astype(BF16)
        windows[k, :, :LP] = high
        windows[k, :, LP:] = (window - high.astype(F32)).astype(BF16)
    sums[...] = jnp.zeros_like(sums)
    lanes = lax.broadcasted_iota(jnp.int32, (LP, 512), 0)
    depths = lax.broadcasted_iota(jnp.int32, (16, 512), 0)

    def one_group(turn, carry):
        rows = pl.ds(pl.multiple_of(turn * GROUP, GROUP), GROUP)
        inside, along, offset, across = [codes[k, rows, :] for k in range(4)]
        kind = groups[rows, :]
        e1, e3 = steps(along), steps(across)
        third = (offset * 43) >> 7
        ninth = (offset * 57) >> 9
        shift = [ninth - 1, third - 3 * ninth - 1, offset - 3 * third - 1]
        lane_a = ((inside >> 5) + 1) * Y + ((inside >> 3) & 3) + 1
        depth_a = (inside & 7) + 2
        lane_b = lane_a + e1[0] * Y + e1[1]
        depth_b = depth_a + e1[2]
        lane_c = lane_a + shift[0] * Y + shift[1]
        depth_c = depth_a + shift[2]
        lane_d = lane_c + e3[0] * Y + e3[1]
        depth_d = depth_c + e3[2]
        lane4 = jnp.concatenate([lane_a, lane_b, lane_c, lane_d], 1)
        depth4 = jnp.concatenate([depth_a, depth_b, depth_c, depth_d], 1)
        places = []
        for t in range(GROUP):
            anchor = base[turn * GROUP + t]
            place = lax.rem(anchor, geo.bz)
            plane = lax.div(anchor, geo.bz)
            corner = 4 * Y * lax.div(plane, geo.by) + 4 * lax.rem(plane, geo.by)
            places.append(place)
            hot = jnp.where(lanes == lane4[t : t + 1] + corner, 1.0, 0.0).astype(BF16)
            hots[t] = hot
            picked = jnp.dot(
                windows[place], jnp.concatenate([hot, hot], 0), preferred_element_type=F32
            )
            mask = depths == depth4[t : t + 1]
            for c in range(3):
                part = jnp.where(mask, picked[16 * c : 16 * c + 16], 0.0)
                gathered[c, t : t + 1, :] = jnp.sum(part, 0, keepdims=True)
        line_one, line_two, apart = [], [], []
        for c in range(3):
            ua, ub, uc, ud = [gathered[c, :, 128 * n : 128 * n + 128] for n in range(4)]
            step1, step3 = e1[c].astype(F32), e3[c].astype(F32)
            line_one.append((ub - ua) + step1)
            line_two.append((ud - uc) + step3)
            lattice = shift[c].astype(F32) + 0.5 * (step3 - step1)
            apart.append(0.5 * ((uc + ud) - (ua + ub)) + lattice)
        square = apart[0] * apart[0] + apart[1] * apart[1] + apart[2] * apart[2] + core_square
        product = (
            line_one[0] * line_two[0] + line_one[1] * line_two[1] + line_one[2] * line_two[2]
        )
        coupling = (0.5 * stiffness) * product / (square * jnp.sqrt(square))
        pieces = []
        for group in (0, 1) if both else (0,):
            chosen = jnp.where(kind == group, coupling, 0.0)
            halves = [split(chosen * apart[c]) for c in range(3)]
            for piece in range(2):
                for c in range(3):
                    h = halves[c][piece]
                    pieces.append(jnp.concatenate([-h, -h, h, h], 1))
        for t in range(GROUP):
            mask = depths == depth4[t : t + 1]
            spread = jnp.concatenate(
                [jnp.where(mask, piece[t : t + 1], 0.0) for piece in pieces], 0
            ).astype(BF16)
            pushed = lax.dot_general(
                spread, hots[t], (((1,), (1,)), ((), ())), preferred_element_type=F32
            )
            for group in range(2 if both else 1):
                part = pushed[96 * group : 96 * group + 48] + pushed[96 * group + 48 : 96 * group + 96]
                sums[group, places[t]] += part
        return carry

    lax.fori_loop(0, geo.tiles // GROUP, one_group, 0)

    def folded(group, c, k):
        rows = jnp.zeros((8, LP), F32)
        if k < geo.bz:
            rows = rows + sums[group, k, 16 * c : 16 * c + 8, :]
        if k > 0:
            rows = rows + sums[group, k - 1, 16 * c + 8 : 16 * c + 16, :]
        return rows

    for c in range(3):
        for k in range(geo.bz + 1):
            rows = slice(8 * k, 8 * k + 8)
            if both:
                frozen[c, rows, :] = folded(1, c, k)
            force[c, rows, :] = folded(0, c, k) + frozen[c, rows, :]


def first_kernel(
    geo, base, flags, face, rows_in, from_low, from_high, codes, groups,
    u, u_old, jinv, frozen, force, zbuf, wide, *work,
):
    targets = [u.at[c] for c in range(3)] + [u_old.at[c] for c in range(3)]
    targets = targets + [jinv.at[c] for c in range(9)]
    fill_done(geo, flags, face, rows_in, from_low, from_high, wide, targets)
    pair_pass(geo, base, u, codes, groups, True, work, frozen, force)
    z_slab(geo, force, zbuf)


def next_kernel(
    geo, base, flags, face, rows_in, from_low, from_high, u, u_old, jinv, frozen, codes, groups,
    new_u, norm, force, zbuf, wide, total, *work,
):
    sum_done(geo, flags, face, rows_in, from_low, from_high, wide, total)
    update(geo, total, u, u_old, jinv, new_u, norm)
    pair_pass(geo, base, new_u, codes, groups, False, work, frozen, force)
    z_slab(geo, force, zbuf)


def last_kernel(
    geo, flags, face, rows_in, from_low, from_high, u, u_old, jinv, norm_0, norm_1,
    out, norms, wide, total, new_u, norm_2,
):
    sum_done(geo, flags, face, rows_in, from_low, from_high, wide, total)
    update(geo, total, u, u_old, jinv, new_u, norm_2)
    for c in range(3):
        wide[...] = new_u[c, 2 : 2 + geo.sz, :].T
        for x in range(geo.sx):
            start = (x + 1) * geo.Y + 1
            out[c, x * geo.sy : (x + 1) * geo.sy, :] = wide[start : start + geo.sy, :]
    lane = lax.broadcasted_iota(jnp.int32, (1, geo.LP), 1)
    line = jnp.zeros((1, geo.LP), F32)
    for k, norm in enumerate((norm_0, norm_1, norm_2)):
        line = line + jnp.where(lane == k, jnp.sum(norm[...]), 0.0)
    norms[...] = jnp.broadcast_to(line, norms.shape)


def ring(shard, axis, by):
    count = lax.axis_size(axis)
    return lax.ppermute(shard, axis, [(i, (i + by) % count) for i in range(count)])


def swap(low_buffer, high_buffer, axis):
    return ring(high_buffer, axis, 1), ring(low_buffer, axis, -1)


def swap_joint(buffer, axis):
    if lax.axis_size(axis) <= 2:
        other = ring(buffer, axis, 1)
        return other, other
    return ring(buffer, axis, 1), ring(buffer, axis, -1)


def per_device(u_old, u_trial, jacobian_inverse, tile_base, pair_codes, pair_groups):
    sx, sy, sz = u_old.shape[1:]
    geo = Geo(sx, sy, sz, tile_base.shape[0])
    if sz != 128 or geo.LP != 128 or sy % 8 or geo.tiles % GROUP:
        raise ValueError("unsupported sizes")
    axes = ("gx", "gy", "gz")
    cells = 3.0 * sx * sy * sz
    devices = 1
    limits = []
    for axis in axes:
        cells = cells * lax.axis_size(axis)
        devices = devices * lax.axis_size(axis)
        at = lax.axis_index(axis)
        limits += [(at > 0).astype(jnp.int32), (at < lax.axis_size(axis) - 1).astype(jnp.int32)]
    flags = jnp.stack(limits)
    vmem, smem = pl.BlockSpec(memory_space=pltpu.VMEM), pl.BlockSpec(memory_space=pltpu.SMEM)

    def arr(*shape):
        return jax.ShapeDtypeStruct(shape, F32)

    def call(kernel, name, scalars, operands, outs, scratch=()):
        return pl.pallas_call(
            functools.partial(kernel, geo),
            out_shape=outs,
            in_specs=[smem] * len(scalars) + [vmem] * len(operands),
            out_specs=[vmem] * len(outs),
            scratch_shapes=list(scratch),
            compiler_params=pltpu.CompilerParams(vmem_limit_bytes=VMEM_GRANT),
            name=name,
        )(*scalars, *operands)

    def spot(*shape, dtype=F32):
        return pltpu.VMEM(shape, dtype)

    def work(count):
        return [
            spot(geo.bz, 48, 2 * geo.LP, dtype=BF16),
            spot(GROUP, geo.LP, 512, dtype=BF16),
            spot(3, GROUP, 512),
            spot(count, geo.bz, 48, geo.LP),
        ]

    square = spot(geo.LP, sz)
    lattice = arr(3, geo.ZR, geo.LP)
    faces3, rows8, zshape = arr(3, geo.RP, sz), arr(8, geo.LP), arr(3, 8, geo.LP)
    slab = arr(3, geo.slab, 128)

    ut = u_trial.reshape(3, sx * sy, sz)
    uo = u_old.reshape(3, sx * sy, sz)
    ji = jacobian_inverse.reshape(9, sx * sy, sz)

    face, zbuf = call(
        fill_z_kernel, "fill_z", [], [ut, uo, ji], [arr(15, geo.RP, sz), arr(32, geo.LP)], [square]
    )
    z_low, z_high = swap_joint(zbuf, "gz")
    wide_x = arr(15 * sy + 32, 128)
    x_low, x_high = call(
        fill_x_kernel, "fill_x", [flags], [ut, uo, ji, z_low, z_high], [wide_x, wide_x]
    )
    from_low, from_high = swap(x_low, x_high, "gx")
    wide_y = arr(fill_y_rows(geo), 128)
    face, rows, y_low, y_high = call(
        fill_y_kernel,
        "fill_y",
        [flags],
        [face, z_low, z_high, from_low, from_high],
        [arr(15, geo.RP, sz), arr(32, geo.LP), wide_y, wide_y],
    )
    from_low, from_high = swap(y_low, y_high, "gy")
    u, uo_l, ji_l, frozen, force, zbuf = call(
        first_kernel,
        "first_pass",
        [tile_base, flags],
        [face, rows, from_low, from_high, pair_codes, pair_groups],
        [lattice, lattice, arr(9, geo.ZR, geo.LP), lattice, lattice, zshape],
        [square] + work(2),
    )

    norm_list = []
    for iteration in range(ITERS):
        z_low, z_high = swap_joint(zbuf, "gz")
        face, rows, x_low, x_high = call(
            sum_x_kernel, "sum_x", [flags], [force, z_low, z_high], [faces3, rows8, slab, slab]
        )
        from_low, from_high = swap(x_low, x_high, "gx")
        face, rows, y_low, y_high = call(
            sum_y_kernel,
            "sum_y",
            [flags],
            [face, rows, from_low, from_high],
            [faces3, rows8, slab, slab],
        )
        from_low, from_high = swap(y_low, y_high, "gy")
        total = spot(3, geo.ZR, geo.LP)
        if iteration < ITERS - 1:
            u, norm, force, zbuf = call(
                next_kernel,
                "next_pass",
                [tile_base, flags],
                [face, rows, from_low, from_high, u, uo_l, ji_l, frozen, pair_codes, pair_groups],
                [lattice, rows8, lattice, zshape],
                [square, total] + work(1),
            )
            norm_list.append(norm)
    out, norms = call(
        last_kernel,
        "last",
        [flags],
        [face, rows, from_low, from_high, u, uo_l, ji_l] + norm_list,
        [arr(3, sx * sy, sz), arr(devices, 128)],
        [square, spot(3, geo.ZR, geo.LP), spot(3, geo.ZR, geo.LP), spot(8, geo.LP)],
    )
    spread = lax.all_to_all(norms.reshape(devices, 1, 128), axes, 0, 0)
    squares = jnp.sum(spread, axis=(0, 1))[:ITERS]
    return out.reshape(3, sx, sy, sz), jnp.sqrt(squares / cells)


def solution(mesh):
    return jax.shard_map(
        per_device,
        mesh=mesh,
        in_specs=(
            P(None, "gx", "gy", "gz"),
            P(None, "gx", "gy", "gz"),
            P(None, None, "gx", "gy", "gz"),
            P(("gx", "gy", "gz")),
            P(None, ("gx", "gy", "gz"), None),
            P(("gx", "gy", "gz"), None),
        ),
        out_specs=(P(None, "gx", "gy", "gz"), P()),
        check_vma=False,
    )
```

```python
import functools

import jax
import jax.numpy as jnp
from jax import lax
from jax.experimental import pallas as pl
from jax.experimental.pallas import tpu as pltpu
from jax.sharding import PartitionSpec as P

ITERS = 3
step_size = 0.5
stiffness = 0.5
core_square = 0.5

F32 = jnp.float32
BF16 = jnp.bfloat16
GROUP = 8
VMEM_GRANT = 12 << 20


class Geo:
    def __init__(self, sx, sy, sz, tiles):
        self.sx, self.sy, self.sz, self.tiles = sx, sy, sz, tiles
        self.X, self.Y = sx + 2, sy + 2
        self.XY = self.X * self.Y
        self.LP = -(-self.XY // 128) * 128
        self.RP = -(-self.XY // 8) * 8
        self.ZR = sz + 8
        self.by = sy // 4
        self.bz = sz // 8
        self.slab = -(-(2 * max(self.X, self.Y) + 2) // 8) * 8


def flag_view(geo, scalars):
    return [scalars[geo.tiles + k] for k in range(6)]


def roll(x, shift, size):
    return pltpu.roll(x, shift % size, 1)


def lane_xy(geo, shape):
    lane = lax.broadcasted_iota(jnp.int32, shape, len(shape) - 1)
    x = jnp.zeros_like(lane)
    for k in range(1, geo.X):
        x = x + (lane >= k * geo.Y).astype(jnp.int32)
    return lane, x, lane - x * geo.Y


def add_rows_x(geo, rows, low, high, has_low, has_high):
    lane, _, _ = lane_xy(geo, rows.shape)
    span = geo.sx * geo.Y
    from_low = roll(low, -span, geo.LP)
    from_high = roll(high, span, geo.LP)
    rows = rows + jnp.where((lane < 2 * geo.Y) & has_low, from_low, 0.0)
    return rows + jnp.where((lane >= span) & (lane < geo.XY) & has_high, from_high, 0.0)


def add_rows_y(geo, rows, low, high, has_low, has_high):
    lane, _, y = lane_xy(geo, rows.shape)
    from_low = roll(low, -geo.sy, geo.LP)
    from_high = roll(high, geo.sy, geo.LP)
    inside = lane < geo.XY
    rows = rows + jnp.where((y < 2) & inside & has_low, from_low, 0.0)
    return rows + jnp.where((y >= geo.sy) & inside & has_high, from_high, 0.0)


def fill_z_kernel(geo, mine, face, zbuf, x_low, x_high, wide):
    wide[...] = jnp.zeros_like(wide)
    zbuf[...] = jnp.zeros_like(zbuf)
    last = (geo.sx - 1) * geo.sy
    for c in range(15):
        for x in range(geo.sx):
            start = (x + 1) * geo.Y + 1
            wide[start : start + geo.sy, :] = mine[c, x * geo.sy : (x + 1) * geo.sy, :]
        x_low[c * geo.sy : (c + 1) * geo.sy, :] = mine[c, 0 : geo.sy, :]
        x_high[c * geo.sy : (c + 1) * geo.sy, :] = mine[c, last : last + geo.sy, :]
        value = wide[...]
        face[c] = value[: geo.RP]
        turned = value.T
        zbuf[c : c + 1, :] = turned[0:1]
        zbuf[16 + c : 17 + c, :] = turned[geo.sz - 1 : geo.sz]


def fill_rows(flags, z_low, z_high):
    low = jnp.where(flags[4] > 0, z_low[16:32, :], 0.0)
    high = jnp.where(flags[5] > 0, z_high[0:16, :], 0.0)
    return jnp.concatenate([low, high], 0)


def fill_x_kernel(geo, scalars, low, high, z_low, z_high, x_low, x_high):
    rows = fill_rows(flag_view(geo, scalars), z_low, z_high)
    count = 15 * geo.sy
    x_low[:count, :] = low[...]
    x_high[:count, :] = high[...]
    x_low[count : count + 32, :] = rows
    x_high[count : count + 32, :] = rows


def fill_y_kernel(geo, scalars, face, z_low, z_high, from_low, from_high, out, rows_out, y_low, y_high):
    flags = flag_view(geo, scalars)
    has_low, has_high = flags[0] > 0, flags[1] > 0
    count = 15 * geo.sy
    rows = add_rows_x(
        geo,
        fill_rows(flags, z_low, z_high),
        from_low[count : count + 32, :],
        from_high[count : count + 32, :],
        has_low,
        has_high,
    )
    rows_out[...] = rows
    out[...] = face[...]
    y_low[...] = jnp.zeros_like(y_low)
    y_high[...] = jnp.zeros_like(y_high)
    top = (geo.sx + 1) * geo.Y + 1
    for c in range(15):
        part = slice(c * geo.sy, (c + 1) * geo.sy)
        out[c, 1 : 1 + geo.sy, :] = jnp.where(has_low, from_low[part, :], 0.0)
        out[c, top : top + geo.sy, :] = jnp.where(has_high, from_high[part, :], 0.0)
        into = slice(c * geo.X, (c + 1) * geo.X)
        y_low[into, :] = out[c, pl.ds(1, geo.X, stride=geo.Y), :]
        y_high[into, :] = out[c, pl.ds(geo.sy, geo.X, stride=geo.Y), :]
    tail = fill_y_rows(geo) - 32
    y_low[tail : tail + 32, :] = rows
    y_high[tail : tail + 32, :] = rows


def fill_y_rows(geo):
    return -(-15 * geo.X // 8) * 8 + 32


def fill_done(geo, flags, face, rows_in, from_low, from_high, wide, targets):
    has_low, has_high = flags[2] > 0, flags[3] > 0
    tail = fill_y_rows(geo) - 32
    rows = add_rows_y(
        geo,
        rows_in[...],
        from_low[tail : tail + 32, :],
        from_high[tail : tail + 32, :],
        has_low,
        has_high,
    )
    wide[...] = jnp.zeros_like(wide)
    for c, target in enumerate(targets):
        wide[: geo.RP, :] = face[c]
        part = slice(c * geo.X, (c + 1) * geo.X)
        wide[pl.ds(0, geo.X, stride=geo.Y), :] = jnp.where(has_low, from_low[part, :], 0.0)
        wide[pl.ds(geo.sy + 1, geo.X, stride=geo.Y), :] = jnp.where(has_high, from_high[part, :], 0.0)
        target[0:8, :] = jnp.zeros((8, geo.LP), F32)
        target[geo.ZR - 8 : geo.ZR, :] = jnp.zeros((8, geo.LP), F32)
        target[2 : 2 + geo.sz, :] = wide[...].T
        target[1:2, :] = rows[c : c + 1]
        target[geo.sz + 2 : geo.sz + 3, :] = rows[16 + c : 17 + c]


def z_slab(geo, force, zbuf):
    zbuf[...] = jnp.zeros_like(zbuf)
    for c in range(3):
        zbuf[c, 0:2, :] = force[c, 1:3, :]
        zbuf[c, 2:4, :] = force[c, geo.sz + 1 : geo.sz + 3, :]


def sum_x_kernel(geo, scalars, force, z_low, z_high, face, rows_out, x_low, x_high):
    flags = flag_view(geo, scalars)
    has_low, has_high = flags[4] > 0, flags[5] > 0
    rows_out[...] = jnp.zeros_like(rows_out)
    x_low[...] = jnp.zeros_like(x_low)
    x_high[...] = jnp.zeros_like(x_high)
    span, two = geo.sx * geo.Y, 2 * geo.Y
    row = lax.broadcasted_iota(jnp.int32, (geo.sz, geo.LP), 0)
    for c in range(3):
        low = jnp.where(has_low, z_low[c, 2:4, :], 0.0)
        high = jnp.where(has_high, z_high[c, 0:2, :], 0.0)
        value = force[c, 2 : 2 + geo.sz, :]
        value = value + jnp.where(row == 0, low[1:2], 0.0)
        value = value + jnp.where(row == geo.sz - 1, high[0:1], 0.0)
        turned = value.T[: geo.RP]
        face[c] = turned
        low_row = force[c, 1:2, :] + low[0:1]
        high_row = force[c, geo.sz + 2 : geo.sz + 3, :] + high[1:2]
        rows_out[c : c + 1, :] = low_row
        rows_out[4 + c : 5 + c, :] = high_row
        x_low[c, 0:two, :] = face[c, 0:two, :]
        x_high[c, 0:two, :] = face[c, span : span + two, :]
        for buffer in (x_low, x_high):
            buffer[c, two : two + 1, :] = low_row
            buffer[c, two + 1 : two + 2, :] = high_row


def slab_rows(buffer, at):
    zero = jnp.zeros_like(buffer[0, at : at + 1, :])
    low = [buffer[c, at : at + 1, :] for c in range(3)]
    high = [buffer[c, at + 1 : at + 2, :] for c in range(3)]
    return jnp.concatenate(low + [zero] + high + [zero], 0)


def sum_y_kernel(geo, scalars, face, rows_in, from_low, from_high, out, rows_out, y_low, y_high):
    flags = flag_view(geo, scalars)
    has_low, has_high = flags[0] > 0, flags[1] > 0
    span, two = geo.sx * geo.Y, 2 * geo.Y
    rows = add_rows_x(
        geo, rows_in[...], slab_rows(from_low, two), slab_rows(from_high, two), has_low, has_high
    )
    rows_out[...] = rows
    out[...] = face[...]
    y_low[...] = jnp.zeros_like(y_low)
    y_high[...] = jnp.zeros_like(y_high)
    for c in range(3):
        out[c, 0:two, :] += jnp.where(has_low, from_low[c, 0:two, :], 0.0)
        out[c, span : span + two, :] += jnp.where(has_high, from_high[c, 0:two, :], 0.0)
        for plane in range(2):
            into = slice(plane * geo.X, (plane + 1) * geo.X)
            y_low[c, into, :] = out[c, pl.ds(plane, geo.X, stride=geo.Y), :]
            y_high[c, into, :] = out[c, pl.ds(geo.sy + plane, geo.X, stride=geo.Y), :]
        at = 2 * geo.X
        for buffer in (y_low, y_high):
            buffer[c, at : at + 1, :] = rows[c : c + 1]
            buffer[c, at + 1 : at + 2, :] = rows[4 + c : 5 + c]


def sum_done(geo, flags, face, rows_in, from_low, from_high, wide, total):
    has_low, has_high = flags[2] > 0, flags[3] > 0
    at = 2 * geo.X
    rows = add_rows_y(
        geo, rows_in[...], slab_rows(from_low, at), slab_rows(from_high, at), has_low, has_high
    )
    wide[...] = jnp.zeros_like(wide)
    for c in range(3):
        wide[: geo.RP, :] = face[c]
        for plane in range(2):
            part = slice(plane * geo.X, (plane + 1) * geo.X)
            low_at = pl.ds(plane, geo.X, stride=geo.Y)
            high_at = pl.ds(geo.sy + plane, geo.X, stride=geo.Y)
            wide[low_at, :] = wide[low_at, :] + jnp.where(has_low, from_low[c, part, :], 0.0)
            wide[high_at, :] = wide[high_at, :] + jnp.where(has_high, from_high[c, part, :], 0.0)
        total[c, 0:8, :] = jnp.zeros((8, geo.LP), F32)
        total[c, geo.ZR - 8 : geo.ZR, :] = jnp.zeros((8, geo.LP), F32)
        total[c, 2 : 2 + geo.sz, :] = wide[...].T
        total[c, 1:2, :] = rows[c : c + 1]
        total[c, geo.sz + 2 : geo.sz + 3, :] = rows[4 + c : 5 + c]


def update(geo, total, u, u_old, jinv, new_u, norm):
    lane, x, y = lane_xy(geo, (8, geo.LP))
    owned = (x >= 1) & (x <= geo.sx) & (y >= 1) & (y <= geo.sy)
    squares = jnp.zeros((8, geo.LP), F32)
    for k in range(geo.ZR // 8):
        rows = slice(8 * k, 8 * k + 8)
        now = [u[c, rows, :] for c in range(3)]
        residual = [now[c] - u_old[c, rows, :] - step_size * total[c, rows, :] for c in range(3)]
        for r in range(3):
            applied = sum(jinv[3 * r + m, rows, :] * residual[m] for m in range(3))
            new_u[r, rows, :] = now[r] - applied
        z = lax.broadcasted_iota(jnp.int32, (8, geo.LP), 0) + (8 * k - 1)
        mask = owned & (z >= 1) & (z <= geo.sz)
        square = residual[0] * residual[0] + residual[1] * residual[1] + residual[2] * residual[2]
        squares = squares + jnp.where(mask, square, 0.0)
    norm[...] = squares


def steps(code):
    which = code >> 1
    direction = 1 - 2 * (code & 1)
    return [jnp.where(which == k, direction, 0) for k in range(3)]


def split(value):
    high = value.astype(BF16).astype(F32)
    return high, value - high


class Codes:
    def __init__(self, geo, codes, rows):
        Y = geo.Y
        inside, along, offset, across = [codes[k, rows, :] for k in range(4)]
        self.e1, self.e3 = e1, e3 = steps(along), steps(across)
        third = (offset * 43) >> 7
        ninth = (offset * 57) >> 9
        self.shift = shift = [ninth - 1, third - 3 * ninth - 1, offset - 3 * third - 1]
        lane_a = ((inside >> 5) + 1) * Y + ((inside >> 3) & 3) + 1
        depth_a = (inside & 7) + 2
        lane_b = lane_a + e1[0] * Y + e1[1]
        depth_b = depth_a + e1[2]
        lane_c = lane_a + shift[0] * Y + shift[1]
        depth_c = depth_a + shift[2]
        lane_d = lane_c + e3[0] * Y + e3[1]
        depth_d = depth_c + e3[2]
        self.lane4 = jnp.concatenate([lane_a, lane_b, lane_c, lane_d], 1)
        self.depth4 = jnp.concatenate([depth_a, depth_b, depth_c, depth_d], 1)


def group_rows(turn):
    if isinstance(turn, int):
        return slice(turn * GROUP, (turn + 1) * GROUP)
    return pl.ds(pl.multiple_of(turn * GROUP, GROUP), GROUP)


def hot_kernel(geo, start, scalars, codes, hots):
    depth = lax.broadcasted_iota(jnp.int32, (16, 512), 0).astype(jnp.int16)
    one, zero = jnp.ones((16, 512), BF16), jnp.zeros((16, 512), BF16)

    def one_group(turn, carry):
        rows = group_rows(turn)
        lane4 = Codes(geo, codes, pl.ds(pl.multiple_of(start + turn * GROUP, GROUP), GROUP)).lane4
        for t in range(GROUP):
            anchor = scalars[start + turn * GROUP + t]
            plane = lax.div(anchor, geo.bz)
            corner = 4 * geo.Y * lax.div(plane, geo.by) + 4 * lax.rem(plane, geo.by)
            lanes = jnp.broadcast_to(lane4[t : t + 1] + corner, (16, 512)).astype(jnp.int16)
            for k in range(geo.LP // 16):
                hit = (lanes - jnp.int16(16 * k)) == depth
                hots[turn * GROUP + t, 16 * k : 16 * k + 16, :] = jnp.where(hit, one, zero)
        return carry

    lax.fori_loop(0, hots.shape[0] // GROUP, one_group, 0)


def pair_pass(geo, scalars, u, hots, codes, groups, both, work, frozen, force):
    windows, pieces, sums = work
    LP = geo.LP
    kinds = (0, 1) if both else (0,)
    for k in range(geo.bz):
        window = u[:, 8 * k : 8 * k + 16, :].reshape(48, LP)
        high = window.astype(BF16)
        windows[k, :, :LP] = high
        windows[k, :, LP:] = (window - high.astype(F32)).astype(BF16)
    sums[...] = jnp.zeros_like(sums)
    depths = lax.broadcasted_iota(jnp.int32, (16, 512), 0)
    def place_of(turn, t):
        return lax.rem(scalars[turn * GROUP + t], geo.bz)

    sub = lax.broadcasted_iota(jnp.int32, (8, 128), 0)
    even = [(sub & step) == 0 for step in (1, 2, 4)]

    def merged(low, high, level):
        keep, step = even[level], 1 << level
        moved = pltpu.roll(jnp.where(keep, high, low), 8 - step, 0)
        return jnp.where(keep, low, high) + moved

    def gather_tile(turn, t, depth4):
        hot = hots[turn * GROUP + t]
        picked = jnp.dot(
            windows[place_of(turn, t)],
            jnp.concatenate([hot, hot], 0),
            preferred_element_type=F32,
        )
        mask = depths == depth4[t : t + 1]
        parts = []
        for c in range(3):
            part = jnp.where(mask, picked[16 * c : 16 * c + 16], 0.0)
            part = part[:8] + part[8:]
            parts += [part[:, 128 * n : 128 * n + 128] for n in range(4)]
        return parts

    def scatter_tile(turn, t, depth4, slot):
        mask = depths == depth4[t : t + 1]
        spread = jnp.concatenate(
            [
                jnp.where(mask, pieces[slot, k, t : t + 1, :], 0.0).astype(BF16)
                for k in range(6 * len(kinds))
            ],
            0,
        )
        pushed = lax.dot_general(
            spread, hots[turn * GROUP + t], (((1,), (1,)), ((), ())), preferred_element_type=F32
        )
        place = place_of(turn, t)
        for group in kinds:
            part = pushed[96 * group : 96 * group + 48] + pushed[96 * group + 48 : 96 * group + 96]
            sums[group, place] += part

    def pair_forces(turn, code, points, slot):
        kind = groups[group_rows(turn), :]
        line_one, line_two, apart = [], [], []
        for c in range(3):
            ua, ub, uc, ud = points[4 * c : 4 * c + 4]
            step1, step3 = code.e1[c].astype(F32), code.e3[c].astype(F32)
            line_one.append((ub - ua) + step1)
            line_two.append((ud - uc) + step3)
            lattice = code.shift[c].astype(F32) + 0.5 * (step3 - step1)
            apart.append(0.5 * ((uc + ud) - (ua + ub)) + lattice)
        square = apart[0] * apart[0] + apart[1] * apart[1] + apart[2] * apart[2] + core_square
        product = (
            line_one[0] * line_two[0] + line_one[1] * line_two[1] + line_one[2] * line_two[2]
        )
        coupling = (0.5 * stiffness) * product / (square * jnp.sqrt(square))
        at = 0
        for group in kinds:
            chosen = jnp.where(kind == group, coupling, 0.0)
            halves = [split(chosen * apart[c]) for c in range(3)]
            for piece in range(2):
                for c in range(3):
                    h = halves[c][piece]
                    pieces[slot, at] = jnp.concatenate([-h, -h, h, h], 1)
                    at += 1

    def one_group(turn, do_scatter, do_gather):
        before = Codes(geo, codes, group_rows(turn - 1)) if do_scatter else None
        code = Codes(geo, codes, group_rows(turn)) if do_gather else None
        waiting = []
        for t in range(GROUP):
            if do_gather:
                parts, level = gather_tile(turn, t, code.depth4), 0
                while (t >> level) & 1:
                    parts = [merged(x, y, level) for x, y in zip(waiting.pop(), parts)]
                    level += 1
                waiting.append(parts)
            if do_scatter:
                scatter_tile(turn - 1, t, before.depth4, (turn - 1) & 1)
        if do_gather:
            pair_forces(turn, code, waiting.pop(), turn & 1)

    def looped(turn, carry):
        one_group(turn, True, True)
        return carry

    count = geo.tiles // GROUP
    one_group(0, False, True)
    lax.fori_loop(1, count, looped, 0)
    one_group(count, True, False)

    def folded(group, c, k):
        rows = jnp.zeros((8, LP), F32)
        if k < geo.bz:
            rows = rows + sums[group, k, 16 * c : 16 * c + 8, :]
        if k > 0:
            rows = rows + sums[group, k - 1, 16 * c + 8 : 16 * c + 16, :]
        return rows

    for c in range(3):
        for k in range(geo.bz + 1):
            rows = slice(8 * k, 8 * k + 8)
            if both:
                frozen[c, rows, :] = folded(1, c, k)
            force[c, rows, :] = folded(0, c, k) + frozen[c, rows, :]


def first_kernel(
    geo, scalars, face, rows_in, from_low, from_high, hots, codes, groups,
    u, u_old, jinv, frozen, force, zbuf, wide, *work,
):
    targets = [u.at[c] for c in range(3)] + [u_old.at[c] for c in range(3)]
    targets = targets + [jinv.at[c] for c in range(9)]
    fill_done(geo, flag_view(geo, scalars), face, rows_in, from_low, from_high, wide, targets)
    pair_pass(geo, scalars, u, hots, codes, groups, True, work, frozen, force)
    z_slab(geo, force, zbuf)


def next_kernel(
    geo, scalars, face, rows_in, from_low, from_high, u, u_old, jinv, frozen, hots, codes, groups,
    new_u, norm, force, zbuf, wide, total, *work,
):
    sum_done(geo, flag_view(geo, scalars), face, rows_in, from_low, from_high, wide, total)
    update(geo, total, u, u_old, jinv, new_u, norm)
    pair_pass(geo, scalars, new_u, hots, codes, groups, False, work, frozen, force)
    z_slab(geo, force, zbuf)


def last_kernel(
    geo, scalars, face, rows_in, from_low, from_high, u, u_old, jinv, norm_0, norm_1,
    out, norms, wide, total, new_u, norm_2,
):
    sum_done(geo, flag_view(geo, scalars), face, rows_in, from_low, from_high, wide, total)
    update(geo, total, u, u_old, jinv, new_u, norm_2)
    for c in range(3):
        wide[...] = new_u[c, 2 : 2 + geo.sz, :].T
        for x in range(geo.sx):
            start = (x + 1) * geo.Y + 1
            out[c, x * geo.sy : (x + 1) * geo.sy, :] = wide[start : start + geo.sy, :]
    lane = lax.broadcasted_iota(jnp.int32, (1, geo.LP), 1)
    line = jnp.zeros((1, geo.LP), F32)
    for k, norm in enumerate((norm_0, norm_1, norm_2)):
        line = line + jnp.where(lane == k, jnp.sum(norm[...]), 0.0)
    norms[...] = jnp.broadcast_to(line, norms.shape)


def ring(shard, axis, by):
    count = lax.axis_size(axis)
    return lax.ppermute(shard, axis, [(i, (i + by) % count) for i in range(count)])


def swap(low_buffer, high_buffer, axis):
    return ring(high_buffer, axis, 1), ring(low_buffer, axis, -1)


def swap_joint(buffer, axis):
    if lax.axis_size(axis) <= 2:
        other = ring(buffer, axis, 1)
        return other, other
    return ring(buffer, axis, 1), ring(buffer, axis, -1)


def per_device(u_old, u_trial, jacobian_inverse, tile_base, pair_codes, pair_groups):
    sx, sy, sz = u_old.shape[1:]
    geo = Geo(sx, sy, sz, tile_base.shape[0])
    if sz != 128 or geo.LP != 128 or sy % 8 or geo.tiles % GROUP:
        raise ValueError("unsupported sizes")
    axes = ("gx", "gy", "gz")
    cells = 3.0 * sx * sy * sz
    devices = 1
    limits = []
    for axis in axes:
        cells = cells * lax.axis_size(axis)
        devices = devices * lax.axis_size(axis)
        at = lax.axis_index(axis)
        limits += [(at > 0).astype(jnp.int32), (at < lax.axis_size(axis) - 1).astype(jnp.int32)]
    scalars = jnp.concatenate([tile_base, jnp.stack(limits)])
    vmem, smem = pl.BlockSpec(memory_space=pltpu.VMEM), pl.BlockSpec(memory_space=pltpu.SMEM)

    def arr(*shape):
        return jax.ShapeDtypeStruct(shape, F32)

    def call(kernel, name, scalars, operands, outs, scratch=(), cost=None, flags=None):
        return pl.pallas_call(
            functools.partial(kernel, geo),
            out_shape=outs,
            in_specs=[smem] * len(scalars) + [vmem] * len(operands),
            out_specs=[vmem] * len(outs),
            scratch_shapes=list(scratch),
            compiler_params=pltpu.CompilerParams(vmem_limit_bytes=VMEM_GRANT, flags=flags),
            cost_estimate=cost,
            name=name,
        )(*scalars, *operands)

    def spot(*shape, dtype=F32):
        return pltpu.VMEM(shape, dtype)

    def work(count):
        return [
            spot(geo.bz, 48, 2 * geo.LP, dtype=BF16),
            spot(2, 6 * count, GROUP, 512),
            spot(count, geo.bz, 48, geo.LP),
        ]

    square = spot(geo.LP, sz)
    lattice = arr(3, geo.ZR, geo.LP)
    faces3, rows8, zshape = arr(3, geo.RP, sz), arr(8, geo.LP), arr(3, 8, geo.LP)
    slab = arr(3, geo.slab, 128)

    ut = u_trial.reshape(3, sx * sy, sz)
    uo = u_old.reshape(3, sx * sy, sz)
    ji = jacobian_inverse.reshape(9, sx * sy, sz)

    hots = call(
        lambda geo, *refs: hot_kernel(geo, 0, *refs),
        "hots",
        [scalars],
        [pair_codes],
        [jax.ShapeDtypeStruct((geo.tiles, geo.LP, 512), BF16)],
        cost=pl.CostEstimate(flops=0, bytes_accessed=16 << 20, transcendentals=0),
    )[0]
    part_x = arr(15 * sy, 128)
    face, zbuf, x_low, x_high = call(
        fill_z_kernel,
        "fill_z",
        [],
        [jnp.concatenate([ut, uo, ji], 0)],
        [arr(15, geo.RP, sz), arr(32, geo.LP), part_x, part_x],
        [square],
    )
    z_low, z_high = swap_joint(zbuf, "gz")
    wide_x = arr(15 * sy + 32, 128)
    x_low, x_high = call(
        fill_x_kernel, "fill_x", [scalars], [x_low, x_high, z_low, z_high], [wide_x, wide_x]
    )
    from_low, from_high = swap(x_low, x_high, "gx")
    wide_y = arr(fill_y_rows(geo), 128)
    face, rows, y_low, y_high = call(
        fill_y_kernel,
        "fill_y",
        [scalars],
        [face, z_low, z_high, from_low, from_high],
        [arr(15, geo.RP, sz), arr(32, geo.LP), wide_y, wide_y],
    )
    from_low, from_high = swap(y_low, y_high, "gy")
    u, uo_l, ji_l, frozen, force, zbuf = call(
        first_kernel,
        "first_pass",
        [scalars],
        [face, rows, from_low, from_high, hots, pair_codes, pair_groups],
        [lattice, lattice, arr(9, geo.ZR, geo.LP), lattice, lattice, zshape],
        [square] + work(2),
    )

    norm_list = []
    for iteration in range(ITERS):
        z_low, z_high = swap_joint(zbuf, "gz")
        face, rows, x_low, x_high = call(
            sum_x_kernel, "sum_x", [scalars], [force, z_low, z_high], [faces3, rows8, slab, slab]
        )
        from_low, from_high = swap(x_low, x_high, "gx")
        face, rows, y_low, y_high = call(
            sum_y_kernel,
            "sum_y",
            [scalars],
            [face, rows, from_low, from_high],
            [faces3, rows8, slab, slab],
        )
        from_low, from_high = swap(y_low, y_high, "gy")
        total = spot(3, geo.ZR, geo.LP)
        if iteration < ITERS - 1:
            u, norm, force, zbuf = call(
                next_kernel,
                "next_pass",
                [scalars],
                [face, rows, from_low, from_high, u, uo_l, ji_l, frozen, hots, pair_codes, pair_groups],
                [lattice, rows8, lattice, zshape],
                [square, total] + work(1),
            )
            norm_list.append(norm)
    out, norms = call(
        last_kernel,
        "last",
        [scalars],
        [face, rows, from_low, from_high, u, uo_l, ji_l] + norm_list,
        [arr(3, sx * sy, sz), arr(devices, 128)],
        [square, spot(3, geo.ZR, geo.LP), spot(3, geo.ZR, geo.LP), spot(8, geo.LP)],
    )
    spread = lax.all_to_all(norms.reshape(devices, 1, 128), axes, 0, 0)
    squares = jnp.sum(spread, axis=(0, 1))[:ITERS]
    return out.reshape(3, sx, sy, sz), jnp.sqrt(squares / cells)


def solution(mesh):
    return jax.shard_map(
        per_device,
        mesh=mesh,
        in_specs=(
            P(None, "gx", "gy", "gz"),
            P(None, "gx", "gy", "gz"),
            P(None, None, "gx", "gy", "gz"),
            P(("gx", "gy", "gz")),
            P(None, ("gx", "gy", "gz"), None),
            P(("gx", "gy", "gz"), None),
        ),
        out_specs=(P(None, "gx", "gy", "gz"), P()),
        check_vma=False,
    )
```

```python
import functools

import jax
import jax.numpy as jnp
from jax import lax
from jax.experimental import pallas as pl
from jax.experimental.pallas import tpu as pltpu
from jax.sharding import PartitionSpec as P

ITERS = 3
step_size = 0.5
stiffness = 0.5
core_square = 0.5

F32 = jnp.float32
BF16 = jnp.bfloat16
GROUP = 8
WINDOW = 64
VMEM_GRANT = 12 << 20


class Geo:
    def __init__(self, sx, sy, sz, tiles):
        self.sx, self.sy, self.sz, self.tiles = sx, sy, sz, tiles
        self.X, self.Y = sx + 2, sy + 2
        self.XY = self.X * self.Y
        self.LP = -(-self.XY // 128) * 128
        self.RP = -(-self.XY // 8) * 8
        self.ZR = sz + 8
        self.bx = sx // 4
        self.by = sy // 4
        self.bz = sz // 8
        self.slab = -(-(2 * max(self.X, self.Y) + 2) // 8) * 8


def flag_view(geo, scalars):
    return [scalars[geo.tiles + k] for k in range(6)]


def roll(x, shift, size):
    return pltpu.roll(x, shift % size, 1)


def lane_xy(geo, shape):
    lane = lax.broadcasted_iota(jnp.int32, shape, len(shape) - 1)
    x = jnp.zeros_like(lane)
    for k in range(1, geo.X):
        x = x + (lane >= k * geo.Y).astype(jnp.int32)
    return lane, x, lane - x * geo.Y


def add_rows_x(geo, rows, low, high, has_low, has_high):
    lane, _, _ = lane_xy(geo, rows.shape)
    span = geo.sx * geo.Y
    from_low = roll(low, -span, geo.LP)
    from_high = roll(high, span, geo.LP)
    rows = rows + jnp.where((lane < 2 * geo.Y) & has_low, from_low, 0.0)
    return rows + jnp.where((lane >= span) & (lane < geo.XY) & has_high, from_high, 0.0)


def add_rows_y(geo, rows, low, high, has_low, has_high):
    lane, _, y = lane_xy(geo, rows.shape)
    from_low = roll(low, -geo.sy, geo.LP)
    from_high = roll(high, geo.sy, geo.LP)
    inside = lane < geo.XY
    rows = rows + jnp.where((y < 2) & inside & has_low, from_low, 0.0)
    return rows + jnp.where((y >= geo.sy) & inside & has_high, from_high, 0.0)


def fill_z_kernel(geo, mine, face, zbuf, x_low, x_high, wide):
    wide[...] = jnp.zeros_like(wide)
    zbuf[...] = jnp.zeros_like(zbuf)
    last = (geo.sx - 1) * geo.sy
    for c in range(15):
        for x in range(geo.sx):
            start = (x + 1) * geo.Y + 1
            wide[start : start + geo.sy, :] = mine[c, x * geo.sy : (x + 1) * geo.sy, :]
        x_low[c * geo.sy : (c + 1) * geo.sy, :] = mine[c, 0 : geo.sy, :]
        x_high[c * geo.sy : (c + 1) * geo.sy, :] = mine[c, last : last + geo.sy, :]
        value = wide[...]
        face[c] = value[: geo.RP]
        turned = value.T
        zbuf[c : c + 1, :] = turned[0:1]
        zbuf[16 + c : 17 + c, :] = turned[geo.sz - 1 : geo.sz]


def fill_rows(flags, z_low, z_high):
    low = jnp.where(flags[4] > 0, z_low[16:32, :], 0.0)
    high = jnp.where(flags[5] > 0, z_high[0:16, :], 0.0)
    return jnp.concatenate([low, high], 0)


def fill_x_kernel(geo, scalars, low, high, z_low, z_high, x_low, x_high):
    rows = fill_rows(flag_view(geo, scalars), z_low, z_high)
    count = 15 * geo.sy
    x_low[:count, :] = low[...]
    x_high[:count, :] = high[...]
    x_low[count : count + 32, :] = rows
    x_high[count : count + 32, :] = rows


def fill_y_kernel(geo, scalars, face, z_low, z_high, from_low, from_high, out, rows_out, y_low, y_high):
    flags = flag_view(geo, scalars)
    has_low, has_high = flags[0] > 0, flags[1] > 0
    count = 15 * geo.sy
    rows = add_rows_x(
        geo,
        fill_rows(flags, z_low, z_high),
        from_low[count : count + 32, :],
        from_high[count : count + 32, :],
        has_low,
        has_high,
    )
    rows_out[...] = rows
    out[...] = face[...]
    y_low[...] = jnp.zeros_like(y_low)
    y_high[...] = jnp.zeros_like(y_high)
    top = (geo.sx + 1) * geo.Y + 1
    for c in range(15):
        part = slice(c * geo.sy, (c + 1) * geo.sy)
        out[c, 1 : 1 + geo.sy, :] = jnp.where(has_low, from_low[part, :], 0.0)
        out[c, top : top + geo.sy, :] = jnp.where(has_high, from_high[part, :], 0.0)
        into = slice(c * geo.X, (c + 1) * geo.X)
        y_low[into, :] = out[c, pl.ds(1, geo.X, stride=geo.Y), :]
        y_high[into, :] = out[c, pl.ds(geo.sy, geo.X, stride=geo.Y), :]
    tail = fill_y_rows(geo) - 32
    y_low[tail : tail + 32, :] = rows
    y_high[tail : tail + 32, :] = rows


def fill_y_rows(geo):
    return -(-15 * geo.X // 8) * 8 + 32


def fill_done(geo, flags, face, rows_in, from_low, from_high, wide, targets):
    has_low, has_high = flags[2] > 0, flags[3] > 0
    tail = fill_y_rows(geo) - 32
    rows = add_rows_y(
        geo,
        rows_in[...],
        from_low[tail : tail + 32, :],
        from_high[tail : tail + 32, :],
        has_low,
        has_high,
    )
    wide[...] = jnp.zeros_like(wide)
    for c, target in enumerate(targets):
        wide[: geo.RP, :] = face[c]
        part = slice(c * geo.X, (c + 1) * geo.X)
        wide[pl.ds(0, geo.X, stride=geo.Y), :] = jnp.where(has_low, from_low[part, :], 0.0)
        wide[pl.ds(geo.sy + 1, geo.X, stride=geo.Y), :] = jnp.where(has_high, from_high[part, :], 0.0)
        target[0:8, :] = jnp.zeros((8, geo.LP), F32)
        target[geo.ZR - 8 : geo.ZR, :] = jnp.zeros((8, geo.LP), F32)
        target[2 : 2 + geo.sz, :] = wide[...].T
        target[1:2, :] = rows[c : c + 1]
        target[geo.sz + 2 : geo.sz + 3, :] = rows[16 + c : 17 + c]


def z_slab(geo, force, zbuf):
    zbuf[...] = jnp.zeros_like(zbuf)
    for c in range(3):
        zbuf[c, 0:2, :] = force[c, 1:3, :]
        zbuf[c, 2:4, :] = force[c, geo.sz + 1 : geo.sz + 3, :]


def sum_x_kernel(geo, scalars, force, z_low, z_high, face, rows_out, x_low, x_high):
    flags = flag_view(geo, scalars)
    has_low, has_high = flags[4] > 0, flags[5] > 0
    rows_out[...] = jnp.zeros_like(rows_out)
    x_low[...] = jnp.zeros_like(x_low)
    x_high[...] = jnp.zeros_like(x_high)
    span, two = geo.sx * geo.Y, 2 * geo.Y
    row = lax.broadcasted_iota(jnp.int32, (geo.sz, geo.LP), 0)
    for c in range(3):
        low = jnp.where(has_low, z_low[c, 2:4, :], 0.0)
        high = jnp.where(has_high, z_high[c, 0:2, :], 0.0)
        value = force[c, 2 : 2 + geo.sz, :]
        value = value + jnp.where(row == 0, low[1:2], 0.0)
        value = value + jnp.where(row == geo.sz - 1, high[0:1], 0.0)
        turned = value.T[: geo.RP]
        face[c] = turned
        low_row = force[c, 1:2, :] + low[0:1]
        high_row = force[c, geo.sz + 2 : geo.sz + 3, :] + high[1:2]
        rows_out[c : c + 1, :] = low_row
        rows_out[4 + c : 5 + c, :] = high_row
        x_low[c, 0:two, :] = face[c, 0:two, :]
        x_high[c, 0:two, :] = face[c, span : span + two, :]
        for buffer in (x_low, x_high):
            buffer[c, two : two + 1, :] = low_row
            buffer[c, two + 1 : two + 2, :] = high_row


def slab_rows(buffer, at):
    zero = jnp.zeros_like(buffer[0, at : at + 1, :])
    low = [buffer[c, at : at + 1, :] for c in range(3)]
    high = [buffer[c, at + 1 : at + 2, :] for c in range(3)]
    return jnp.concatenate(low + [zero] + high + [zero], 0)


def sum_y_kernel(geo, scalars, face, rows_in, from_low, from_high, out, rows_out, y_low, y_high):
    flags = flag_view(geo, scalars)
    has_low, has_high = flags[0] > 0, flags[1] > 0
    span, two = geo.sx * geo.Y, 2 * geo.Y
    rows = add_rows_x(
        geo, rows_in[...], slab_rows(from_low, two), slab_rows(from_high, two), has_low, has_high
    )
    rows_out[...] = rows
    out[...] = face[...]
    y_low[...] = jnp.zeros_like(y_low)
    y_high[...] = jnp.zeros_like(y_high)
    for c in range(3):
        out[c, 0:two, :] += jnp.where(has_low, from_low[c, 0:two, :], 0.0)
        out[c, span : span + two, :] += jnp.where(has_high, from_high[c, 0:two, :], 0.0)
        for plane in range(2):
            into = slice(plane * geo.X, (plane + 1) * geo.X)
            y_low[c, into, :] = out[c, pl.ds(plane, geo.X, stride=geo.Y), :]
            y_high[c, into, :] = out[c, pl.ds(geo.sy + plane, geo.X, stride=geo.Y), :]
        at = 2 * geo.X
        for buffer in (y_low, y_high):
            buffer[c, at : at + 1, :] = rows[c : c + 1]
            buffer[c, at + 1 : at + 2, :] = rows[4 + c : 5 + c]


def sum_done(geo, flags, face, rows_in, from_low, from_high, wide, total):
    has_low, has_high = flags[2] > 0, flags[3] > 0
    at = 2 * geo.X
    rows = add_rows_y(
        geo, rows_in[...], slab_rows(from_low, at), slab_rows(from_high, at), has_low, has_high
    )
    wide[...] = jnp.zeros_like(wide)
    for c in range(3):
        wide[: geo.RP, :] = face[c]
        for plane in range(2):
            part = slice(plane * geo.X, (plane + 1) * geo.X)
            low_at = pl.ds(plane, geo.X, stride=geo.Y)
            high_at = pl.ds(geo.sy + plane, geo.X, stride=geo.Y)
            wide[low_at, :] = wide[low_at, :] + jnp.where(has_low, from_low[c, part, :], 0.0)
            wide[high_at, :] = wide[high_at, :] + jnp.where(has_high, from_high[c, part, :], 0.0)
        total[c, 0:8, :] = jnp.zeros((8, geo.LP), F32)
        total[c, geo.ZR - 8 : geo.ZR, :] = jnp.zeros((8, geo.LP), F32)
        total[c, 2 : 2 + geo.sz, :] = wide[...].T
        total[c, 1:2, :] = rows[c : c + 1]
        total[c, geo.sz + 2 : geo.sz + 3, :] = rows[4 + c : 5 + c]


def update(geo, total, u, u_old, jinv, new_u, norm):
    lane, x, y = lane_xy(geo, (8, geo.LP))
    owned = (x >= 1) & (x <= geo.sx) & (y >= 1) & (y <= geo.sy)
    squares = jnp.zeros((8, geo.LP), F32)
    for k in range(geo.ZR // 8):
        rows = slice(8 * k, 8 * k + 8)
        now = [u[c, rows, :] for c in range(3)]
        residual = [now[c] - u_old[c, rows, :] - step_size * total[c, rows, :] for c in range(3)]
        for r in range(3):
            applied = sum(jinv[3 * r + m, rows, :] * residual[m] for m in range(3))
            new_u[r, rows, :] = now[r] - applied
        z = lax.broadcasted_iota(jnp.int32, (8, geo.LP), 0) + (8 * k - 1)
        mask = owned & (z >= 1) & (z <= geo.sz)
        square = residual[0] * residual[0] + residual[1] * residual[1] + residual[2] * residual[2]
        squares = squares + jnp.where(mask, square, 0.0)
    norm[...] = squares


def steps(code):
    which = code >> 1
    direction = 1 - 2 * (code & 1)
    return [jnp.where(which == k, direction, 0) for k in range(3)]


def split(value):
    high = value.astype(BF16).astype(F32)
    return high, value - high


class Codes:
    def __init__(self, geo, codes, rows):
        Y = 8
        inside, along, offset, across = [codes[k, rows, :] for k in range(4)]
        self.e1, self.e3 = e1, e3 = steps(along), steps(across)
        third = (offset * 43) >> 7
        ninth = (offset * 57) >> 9
        self.shift = shift = [ninth - 1, third - 3 * ninth - 1, offset - 3 * third - 1]
        lane_a = ((inside >> 5) + 2) * Y + ((inside >> 3) & 3) + 2
        depth_a = (inside & 7) + 2
        lane_b = lane_a + e1[0] * Y + e1[1]
        depth_b = depth_a + e1[2]
        lane_c = lane_a + shift[0] * Y + shift[1]
        depth_c = depth_a + shift[2]
        lane_d = lane_c + e3[0] * Y + e3[1]
        depth_d = depth_c + e3[2]
        self.lane4 = jnp.concatenate([lane_a, lane_b, lane_c, lane_d], 1)
        self.depth4 = jnp.concatenate([depth_a, depth_b, depth_c, depth_d], 1)


def group_rows(turn):
    if isinstance(turn, int):
        return slice(turn * GROUP, (turn + 1) * GROUP)
    return pl.ds(pl.multiple_of(turn * GROUP, GROUP), GROUP)


def hot_kernel(geo, codes, hots):
    depth = lax.broadcasted_iota(jnp.int32, (16, 512), 0).astype(jnp.int16)
    one, zero = jnp.ones((16, 512), BF16), jnp.zeros((16, 512), BF16)

    def one_group(turn, carry):
        lane4 = Codes(geo, codes, group_rows(turn)).lane4
        for t in range(GROUP):
            lanes = jnp.broadcast_to(lane4[t : t + 1], (16, 512)).astype(jnp.int16)
            for k in range(WINDOW // 16):
                hit = (lanes - jnp.int16(16 * k)) == depth
                hots[turn * GROUP + t, 16 * k : 16 * k + 16, :] = jnp.where(hit, one, zero)
        return carry

    lax.fori_loop(0, hots.shape[0] // GROUP, one_group, 0)


def pair_pass(geo, scalars, u, hots, codes, groups, both, work, frozen, force):
    windows, pieces, sums, lanes = work
    LP, ZR = geo.LP, geo.ZR
    planes = geo.bx * geo.by
    kinds = (0, 1) if both else (0,)
    gates = window_gates(geo)
    whole = u[...].reshape(3 * ZR, LP)
    high = whole.astype(BF16)
    low = (whole - high.astype(F32)).astype(BF16)
    for plane in range(planes):
        gate = gates[:, WINDOW * plane : WINDOW * (plane + 1)]
        zero = jnp.zeros_like(gate)
        gate = jnp.concatenate(
            [jnp.concatenate([gate, zero], 1), jnp.concatenate([zero, gate], 1)], 0
        ).astype(BF16)
        lanes[0] = jnp.dot(jnp.concatenate([high, low], 1), gate, preferred_element_type=F32)
        for k in range(geo.bz):
            for c in range(3):
                rows = slice(ZR * c + 8 * k, ZR * c + 8 * k + 16)
                windows[geo.bz * plane + k, 16 * c : 16 * c + 16, :] = lanes[0, rows, :].astype(BF16)
    sums[...] = jnp.zeros_like(sums)
    depths = lax.broadcasted_iota(jnp.int32, (16, 512), 0)
    def place_of(turn, t):
        return scalars[turn * GROUP + t]

    sub = lax.broadcasted_iota(jnp.int32, (8, 128), 0)
    even = [(sub & step) == 0 for step in (1, 2, 4)]

    def merged(low, high, level):
        keep, step = even[level], 1 << level
        moved = pltpu.roll(jnp.where(keep, high, low), 8 - step, 0)
        return jnp.where(keep, low, high) + moved

    def gather_tile(turn, t, depth4):
        hot = hots[turn * GROUP + t]
        picked = jnp.dot(
            windows[place_of(turn, t)],
            jnp.concatenate([hot, hot], 0),
            preferred_element_type=F32,
        )
        mask = depths == depth4[t : t + 1]
        parts = []
        for c in range(3):
            part = jnp.where(mask, picked[16 * c : 16 * c + 16], 0.0)
            part = part[:8] + part[8:]
            parts += [part[:, 128 * n : 128 * n + 128] for n in range(4)]
        return parts

    def scatter_tile(turn, t, depth4, slot):
        mask = depths == depth4[t : t + 1]
        spread = jnp.concatenate(
            [
                jnp.where(mask, pieces[slot, k, t : t + 1, :], 0.0).astype(BF16)
                for k in range(6 * len(kinds))
            ],
            0,
        )
        pushed = lax.dot_general(
            spread, hots[turn * GROUP + t], (((1,), (1,)), ((), ())), preferred_element_type=F32
        )
        place = place_of(turn, t)
        for group in kinds:
            part = pushed[96 * group : 96 * group + 48] + pushed[96 * group + 48 : 96 * group + 96]
            sums[group, place] += part

    def pair_forces(turn, code, points, slot):
        kind = groups[group_rows(turn), :]
        line_one, line_two, apart = [], [], []
        for c in range(3):
            ua, ub, uc, ud = points[4 * c : 4 * c + 4]
            step1, step3 = code.e1[c].astype(F32), code.e3[c].astype(F32)
            line_one.append((ub - ua) + step1)
            line_two.append((ud - uc) + step3)
            lattice = code.shift[c].astype(F32) + 0.5 * (step3 - step1)
            apart.append(0.5 * ((uc + ud) - (ua + ub)) + lattice)
        square = apart[0] * apart[0] + apart[1] * apart[1] + apart[2] * apart[2] + core_square
        product = (
            line_one[0] * line_two[0] + line_one[1] * line_two[1] + line_one[2] * line_two[2]
        )
        coupling = (0.5 * stiffness) * product / (square * jnp.sqrt(square))
        at = 0
        for group in kinds:
            chosen = jnp.where(kind == group, coupling, 0.0)
            halves = [split(chosen * apart[c]) for c in range(3)]
            for piece in range(2):
                for c in range(3):
                    h = halves[c][piece]
                    pieces[slot, at] = jnp.concatenate([-h, -h, h, h], 1)
                    at += 1

    def one_group(turn, do_scatter, do_gather):
        before = Codes(geo, codes, group_rows(turn - 1)) if do_scatter else None
        code = Codes(geo, codes, group_rows(turn)) if do_gather else None
        waiting = []
        for t in range(GROUP):
            if do_gather:
                parts, level = gather_tile(turn, t, code.depth4), 0
                while (t >> level) & 1:
                    parts = [merged(x, y, level) for x, y in zip(waiting.pop(), parts)]
                    level += 1
                waiting.append(parts)
            if do_scatter:
                scatter_tile(turn - 1, t, before.depth4, (turn - 1) & 1)
        if do_gather:
            pair_forces(turn, code, waiting.pop(), turn & 1)

    def looped(turn, carry):
        one_group(turn, True, True)
        return carry

    count = geo.tiles // GROUP
    one_group(0, False, True)
    lax.fori_loop(1, count, looped, 0)
    one_group(count, True, False)

    gates = gates.astype(BF16)

    def folded(group):
        for c in range(3):
            for k in range(geo.bz + 1):
                parts = []
                for plane in range(planes):
                    rows = jnp.zeros((8, WINDOW), F32)
                    at = geo.bz * plane + k
                    if k < geo.bz:
                        rows = rows + sums[group, at, 16 * c : 16 * c + 8, :]
                    if k > 0:
                        rows = rows + sums[group, at - 1, 16 * c + 8 : 16 * c + 16, :]
                    parts.append(rows)
                rows = slice(ZR * c + 8 * k, ZR * c + 8 * k + 8)
                for pair in range(0, planes, 2):
                    lanes[pair // 2, rows, :] = jnp.concatenate(parts[pair : pair + 2], 1)
        value = jnp.zeros((3 * ZR, LP), F32)
        for pair in range(planes // 2):
            gate = gates[:, 128 * pair : 128 * pair + 128]
            for piece in split(lanes[pair]):
                value = value + lax.dot_general(
                    piece.astype(BF16), gate, (((1,), (1,)), ((), ())), preferred_element_type=F32
                )
        return value.reshape(3, ZR, LP)

    if both:
        frozen[...] = folded(1)
    force[...] = folded(0) + frozen[...]


def window_gates(geo):
    shape = (geo.LP, WINDOW * geo.bx * geo.by)
    lane = lax.broadcasted_iota(jnp.int32, shape, 0)
    column = lax.broadcasted_iota(jnp.int32, shape, 1)
    plane, cell = column // WINDOW, column % WINDOW
    x = 4 * (plane // geo.by) - 1 + cell // 8
    y = 4 * (plane % geo.by) - 1 + cell % 8
    inside = (x >= 0) & (x < geo.X) & (y >= 0) & (y < geo.Y)
    return jnp.where(inside & (lane == x * geo.Y + y), 1.0, 0.0)


def first_kernel(
    geo, scalars, face, rows_in, from_low, from_high, hots, codes, groups,
    u, u_old, jinv, frozen, force, zbuf, wide, *work,
):
    targets = [u.at[c] for c in range(3)] + [u_old.at[c] for c in range(3)]
    targets = targets + [jinv.at[c] for c in range(9)]
    fill_done(geo, flag_view(geo, scalars), face, rows_in, from_low, from_high, wide, targets)
    pair_pass(geo, scalars, u, hots, codes, groups, True, work, frozen, force)
    z_slab(geo, force, zbuf)


def next_kernel(
    geo, scalars, face, rows_in, from_low, from_high, u, u_old, jinv, frozen, hots, codes, groups,
    new_u, norm, force, zbuf, wide, total, *work,
):
    sum_done(geo, flag_view(geo, scalars), face, rows_in, from_low, from_high, wide, total)
    update(geo, total, u, u_old, jinv, new_u, norm)
    pair_pass(geo, scalars, new_u, hots, codes, groups, False, work, frozen, force)
    z_slab(geo, force, zbuf)


def last_kernel(
    geo, scalars, face, rows_in, from_low, from_high, u, u_old, jinv, norm_0, norm_1,
    out, norms, wide, total, new_u, norm_2,
):
    sum_done(geo, flag_view(geo, scalars), face, rows_in, from_low, from_high, wide, total)
    update(geo, total, u, u_old, jinv, new_u, norm_2)
    for c in range(3):
        wide[...] = new_u[c, 2 : 2 + geo.sz, :].T
        for x in range(geo.sx):
            start = (x + 1) * geo.Y + 1
            out[c, x * geo.sy : (x + 1) * geo.sy, :] = wide[start : start + geo.sy, :]
    lane = lax.broadcasted_iota(jnp.int32, (1, geo.LP), 1)
    line = jnp.zeros((1, geo.LP), F32)
    for k, norm in enumerate((norm_0, norm_1, norm_2)):
        line = line + jnp.where(lane == k, jnp.sum(norm[...]), 0.0)
    norms[...] = jnp.broadcast_to(line, norms.shape)


def ring(shard, axis, by):
    count = lax.axis_size(axis)
    return lax.ppermute(shard, axis, [(i, (i + by) % count) for i in range(count)])


def swap(low_buffer, high_buffer, axis):
    return ring(high_buffer, axis, 1), ring(low_buffer, axis, -1)


def swap_joint(buffer, axis):
    if lax.axis_size(axis) <= 2:
        other = ring(buffer, axis, 1)
        return other, other
    return ring(buffer, axis, 1), ring(buffer, axis, -1)


def per_device(u_old, u_trial, jacobian_inverse, tile_base, pair_codes, pair_groups):
    sx, sy, sz = u_old.shape[1:]
    geo = Geo(sx, sy, sz, tile_base.shape[0])
    if sz != 128 or geo.LP != 128 or sy % 8 or geo.bx % 2 or geo.tiles % GROUP:
        raise ValueError("unsupported sizes")
    axes = ("gx", "gy", "gz")
    cells = 3.0 * sx * sy * sz
    devices = 1
    limits = []
    for axis in axes:
        cells = cells * lax.axis_size(axis)
        devices = devices * lax.axis_size(axis)
        at = lax.axis_index(axis)
        limits += [(at > 0).astype(jnp.int32), (at < lax.axis_size(axis) - 1).astype(jnp.int32)]
    scalars = jnp.concatenate([tile_base, jnp.stack(limits)])
    vmem, smem = pl.BlockSpec(memory_space=pltpu.VMEM), pl.BlockSpec(memory_space=pltpu.SMEM)

    def arr(*shape):
        return jax.ShapeDtypeStruct(shape, F32)

    def call(kernel, name, scalars, operands, outs, scratch=(), cost=None, flags=None):
        return pl.pallas_call(
            functools.partial(kernel, geo),
            out_shape=outs,
            in_specs=[smem] * len(scalars) + [vmem] * len(operands),
            out_specs=[vmem] * len(outs),
            scratch_shapes=list(scratch),
            compiler_params=pltpu.CompilerParams(vmem_limit_bytes=VMEM_GRANT, flags=flags),
            cost_estimate=cost,
            name=name,
        )(*scalars, *operands)

    def spot(*shape, dtype=F32):
        return pltpu.VMEM(shape, dtype)

    anchors = geo.bx * geo.by * geo.bz

    def work(count):
        return [
            spot(anchors, 48, 2 * WINDOW, dtype=BF16),
            spot(2, 6 * count, GROUP, 512),
            spot(count, anchors, 48, WINDOW),
            spot(geo.bx * geo.by // 2, 3 * geo.ZR, geo.LP),
        ]

    square = spot(geo.LP, sz)
    lattice = arr(3, geo.ZR, geo.LP)
    faces3, rows8, zshape = arr(3, geo.RP, sz), arr(8, geo.LP), arr(3, 8, geo.LP)
    slab = arr(3, geo.slab, 128)

    ut = u_trial.reshape(3, sx * sy, sz)
    uo = u_old.reshape(3, sx * sy, sz)
    ji = jacobian_inverse.reshape(9, sx * sy, sz)

    hots = call(
        hot_kernel,
        "hots",
        [],
        [pair_codes],
        [jax.ShapeDtypeStruct((geo.tiles, WINDOW, 512), BF16)],
        cost=pl.CostEstimate(flops=0, bytes_accessed=16 << 20, transcendentals=0),
    )[0]
    part_x = arr(15 * sy, 128)
    face, zbuf, x_low, x_high = call(
        fill_z_kernel,
        "fill_z",
        [],
        [jnp.concatenate([ut, uo, ji], 0)],
        [arr(15, geo.RP, sz), arr(32, geo.LP), part_x, part_x],
        [square],
    )
    z_low, z_high = swap_joint(zbuf, "gz")
    wide_x = arr(15 * sy + 32, 128)
    x_low, x_high = call(
        fill_x_kernel, "fill_x", [scalars], [x_low, x_high, z_low, z_high], [wide_x, wide_x]
    )
    from_low, from_high = swap(x_low, x_high, "gx")
    wide_y = arr(fill_y_rows(geo), 128)
    face, rows, y_low, y_high = call(
        fill_y_kernel,
        "fill_y",
        [scalars],
        [face, z_low, z_high, from_low, from_high],
        [arr(15, geo.RP, sz), arr(32, geo.LP), wide_y, wide_y],
    )
    from_low, from_high = swap(y_low, y_high, "gy")
    u, uo_l, ji_l, frozen, force, zbuf = call(
        first_kernel,
        "first_pass",
        [scalars],
        [face, rows, from_low, from_high, hots, pair_codes, pair_groups],
        [lattice, lattice, arr(9, geo.ZR, geo.LP), lattice, lattice, zshape],
        [square] + work(2),
    )

    norm_list = []
    for iteration in range(ITERS):
        z_low, z_high = swap_joint(zbuf, "gz")
        face, rows, x_low, x_high = call(
            sum_x_kernel, "sum_x", [scalars], [force, z_low, z_high], [faces3, rows8, slab, slab]
        )
        from_low, from_high = swap(x_low, x_high, "gx")
        face, rows, y_low, y_high = call(
            sum_y_kernel,
            "sum_y",
            [scalars],
            [face, rows, from_low, from_high],
            [faces3, rows8, slab, slab],
        )
        from_low, from_high = swap(y_low, y_high, "gy")
        total = spot(3, geo.ZR, geo.LP)
        if iteration < ITERS - 1:
            u, norm, force, zbuf = call(
                next_kernel,
                "next_pass",
                [scalars],
                [face, rows, from_low, from_high, u, uo_l, ji_l, frozen, hots, pair_codes, pair_groups],
                [lattice, rows8, lattice, zshape],
                [square, total] + work(1),
            )
            norm_list.append(norm)
    out, norms = call(
        last_kernel,
        "last",
        [scalars],
        [face, rows, from_low, from_high, u, uo_l, ji_l] + norm_list,
        [arr(3, sx * sy, sz), arr(devices, 128)],
        [square, spot(3, geo.ZR, geo.LP), spot(3, geo.ZR, geo.LP), spot(8, geo.LP)],
    )
    spread = lax.all_to_all(norms.reshape(devices, 1, 128), axes, 0, 0)
    squares = jnp.sum(spread, axis=(0, 1))[:ITERS]
    return out.reshape(3, sx, sy, sz), jnp.sqrt(squares / cells)


def solution(mesh):
    return jax.shard_map(
        per_device,
        mesh=mesh,
        in_specs=(
            P(None, "gx", "gy", "gz"),
            P(None, "gx", "gy", "gz"),
            P(None, None, "gx", "gy", "gz"),
            P(("gx", "gy", "gz")),
            P(None, ("gx", "gy", "gz"), None),
            P(("gx", "gy", "gz"), None),
        ),
        out_specs=(P(None, "gx", "gy", "gz"), P()),
        check_vma=False,
    )
```

```python
import functools

import jax
import jax.numpy as jnp
from jax import lax
from jax.experimental import pallas as pl
from jax.experimental.pallas import tpu as pltpu
from jax.sharding import PartitionSpec as P

ITERS = 3
step_size = 0.5
stiffness = 0.5
core_square = 0.5

F32 = jnp.float32
BF16 = jnp.bfloat16
GROUP = 8
WINDOW = 64
AHEAD = 0
VMEM_GRANT = 12 << 20


class Geo:
    def __init__(self, sx, sy, sz, tiles):
        self.sx, self.sy, self.sz, self.tiles = sx, sy, sz, tiles
        self.X, self.Y = sx + 2, sy + 2
        self.XY = self.X * self.Y
        self.LP = -(-self.XY // 128) * 128
        self.RP = -(-self.XY // 8) * 8
        self.ZR = sz + 8
        self.bx = sx // 4
        self.by = sy // 4
        self.bz = sz // 8
        self.slab = -(-(2 * max(self.X, self.Y) + 2) // 8) * 8


def edges():
    found = []
    for axis in ("gx", "gy", "gz"):
        at = lax.axis_index(axis)
        found += [at > 0, at < lax.axis_size(axis) - 1]
    return found


def roll(x, shift, size):
    return pltpu.roll(x, shift % size, 1)


def lane_xy(geo, shape):
    lane = lax.broadcasted_iota(jnp.int32, shape, len(shape) - 1)
    x = jnp.zeros_like(lane)
    for k in range(1, geo.X):
        x = x + (lane >= k * geo.Y).astype(jnp.int32)
    return lane, x, lane - x * geo.Y


def add_rows_x(geo, rows, low, high, has_low, has_high):
    lane, _, _ = lane_xy(geo, rows.shape)
    span = geo.sx * geo.Y
    from_low = roll(low, -span, geo.LP)
    from_high = roll(high, span, geo.LP)
    rows = rows + jnp.where((lane < 2 * geo.Y) & has_low, from_low, 0.0)
    return rows + jnp.where((lane >= span) & (lane < geo.XY) & has_high, from_high, 0.0)


def add_rows_y(geo, rows, low, high, has_low, has_high):
    lane, _, y = lane_xy(geo, rows.shape)
    from_low = roll(low, -geo.sy, geo.LP)
    from_high = roll(high, geo.sy, geo.LP)
    inside = lane < geo.XY
    rows = rows + jnp.where((y < 2) & inside & has_low, from_low, 0.0)
    return rows + jnp.where((y >= geo.sy) & inside & has_high, from_high, 0.0)


def fill_z_kernel(geo, mine, face, zbuf, x_low, x_high, wide):
    wide[...] = jnp.zeros_like(wide)
    zbuf[...] = jnp.zeros_like(zbuf)
    last = (geo.sx - 1) * geo.sy
    for c in range(15):
        for x in range(geo.sx):
            start = (x + 1) * geo.Y + 1
            wide[start : start + geo.sy, :] = mine[c, x * geo.sy : (x + 1) * geo.sy, :]
        x_low[c * geo.sy : (c + 1) * geo.sy, :] = mine[c, 0 : geo.sy, :]
        x_high[c * geo.sy : (c + 1) * geo.sy, :] = mine[c, last : last + geo.sy, :]
        value = wide[...]
        face[c] = value[: geo.RP]
        turned = value.T
        zbuf[c : c + 1, :] = turned[0:1]
        zbuf[16 + c : 17 + c, :] = turned[geo.sz - 1 : geo.sz]


def fill_rows(flags, z_low, z_high):
    low = jnp.where(flags[4], z_low[16:32, :], 0.0)
    high = jnp.where(flags[5], z_high[0:16, :], 0.0)
    return jnp.concatenate([low, high], 0)


def fill_x_kernel(geo, low, high, z_low, z_high, x_low, x_high):
    rows = fill_rows(edges(), z_low, z_high)
    count = 15 * geo.sy
    x_low[:count, :] = low[...]
    x_high[:count, :] = high[...]
    x_low[count : count + 32, :] = rows
    x_high[count : count + 32, :] = rows


def fill_y_kernel(geo, face, z_low, z_high, from_low, from_high, out, rows_out, y_low, y_high):
    flags = edges()
    has_low, has_high = flags[0], flags[1]
    count = 15 * geo.sy
    rows = add_rows_x(
        geo,
        fill_rows(flags, z_low, z_high),
        from_low[count : count + 32, :],
        from_high[count : count + 32, :],
        has_low,
        has_high,
    )
    rows_out[...] = rows
    out[...] = face[...]
    y_low[...] = jnp.zeros_like(y_low)
    y_high[...] = jnp.zeros_like(y_high)
    top = (geo.sx + 1) * geo.Y + 1
    for c in range(15):
        part = slice(c * geo.sy, (c + 1) * geo.sy)
        out[c, 1 : 1 + geo.sy, :] = jnp.where(has_low, from_low[part, :], 0.0)
        out[c, top : top + geo.sy, :] = jnp.where(has_high, from_high[part, :], 0.0)
        into = slice(c * geo.X, (c + 1) * geo.X)
        y_low[into, :] = out[c, pl.ds(1, geo.X, stride=geo.Y), :]
        y_high[into, :] = out[c, pl.ds(geo.sy, geo.X, stride=geo.Y), :]
    tail = fill_y_rows(geo) - 32
    y_low[tail : tail + 32, :] = rows
    y_high[tail : tail + 32, :] = rows


def fill_y_rows(geo):
    return -(-15 * geo.X // 8) * 8 + 32


def fill_done(geo, flags, face, rows_in, from_low, from_high, wide, targets):
    has_low, has_high = flags[2], flags[3]
    tail = fill_y_rows(geo) - 32
    rows = add_rows_y(
        geo,
        rows_in[...],
        from_low[tail : tail + 32, :],
        from_high[tail : tail + 32, :],
        has_low,
        has_high,
    )
    wide[...] = jnp.zeros_like(wide)
    for c, target in enumerate(targets):
        wide[: geo.RP, :] = face[c]
        part = slice(c * geo.X, (c + 1) * geo.X)
        wide[pl.ds(0, geo.X, stride=geo.Y), :] = jnp.where(has_low, from_low[part, :], 0.0)
        wide[pl.ds(geo.sy + 1, geo.X, stride=geo.Y), :] = jnp.where(has_high, from_high[part, :], 0.0)
        target[0:8, :] = jnp.zeros((8, geo.LP), F32)
        target[geo.ZR - 8 : geo.ZR, :] = jnp.zeros((8, geo.LP), F32)
        target[2 : 2 + geo.sz, :] = wide[...].T
        target[1:2, :] = rows[c : c + 1]
        target[geo.sz + 2 : geo.sz + 3, :] = rows[16 + c : 17 + c]


def z_slab(geo, force, zbuf):
    zbuf[...] = jnp.zeros_like(zbuf)
    for c in range(3):
        zbuf[c, 0:2, :] = force[c, 1:3, :]
        zbuf[c, 2:4, :] = force[c, geo.sz + 1 : geo.sz + 3, :]


def sum_x_kernel(geo, force, z_low, z_high, face, rows_out, x_low, x_high):
    flags = edges()
    has_low, has_high = flags[4], flags[5]
    rows_out[...] = jnp.zeros_like(rows_out)
    x_low[...] = jnp.zeros_like(x_low)
    x_high[...] = jnp.zeros_like(x_high)
    span, two = geo.sx * geo.Y, 2 * geo.Y
    row = lax.broadcasted_iota(jnp.int32, (geo.sz, geo.LP), 0)
    for c in range(3):
        low = jnp.where(has_low, z_low[c, 2:4, :], 0.0)
        high = jnp.where(has_high, z_high[c, 0:2, :], 0.0)
        value = force[c, 2 : 2 + geo.sz, :]
        value = value + jnp.where(row == 0, low[1:2], 0.0)
        value = value + jnp.where(row == geo.sz - 1, high[0:1], 0.0)
        turned = value.T[: geo.RP]
        face[c] = turned
        low_row = force[c, 1:2, :] + low[0:1]
        high_row = force[c, geo.sz + 2 : geo.sz + 3, :] + high[1:2]
        rows_out[c : c + 1, :] = low_row
        rows_out[4 + c : 5 + c, :] = high_row
        x_low[c, 0:two, :] = face[c, 0:two, :]
        x_high[c, 0:two, :] = face[c, span : span + two, :]
        for buffer in (x_low, x_high):
            buffer[c, two : two + 1, :] = low_row
            buffer[c, two + 1 : two + 2, :] = high_row


def slab_rows(buffer, at):
    zero = jnp.zeros_like(buffer[0, at : at + 1, :])
    low = [buffer[c, at : at + 1, :] for c in range(3)]
    high = [buffer[c, at + 1 : at + 2, :] for c in range(3)]
    return jnp.concatenate(low + [zero] + high + [zero], 0)


def sum_y_kernel(geo, face, rows_in, from_low, from_high, out, rows_out, y_low, y_high):
    flags = edges()
    has_low, has_high = flags[0], flags[1]
    span, two = geo.sx * geo.Y, 2 * geo.Y
    rows = add_rows_x(
        geo, rows_in[...], slab_rows(from_low, two), slab_rows(from_high, two), has_low, has_high
    )
    rows_out[...] = rows
    out[...] = face[...]
    y_low[...] = jnp.zeros_like(y_low)
    y_high[...] = jnp.zeros_like(y_high)
    for c in range(3):
        out[c, 0:two, :] += jnp.where(has_low, from_low[c, 0:two, :], 0.0)
        out[c, span : span + two, :] += jnp.where(has_high, from_high[c, 0:two, :], 0.0)
        for plane in range(2):
            into = slice(plane * geo.X, (plane + 1) * geo.X)
            y_low[c, into, :] = out[c, pl.ds(plane, geo.X, stride=geo.Y), :]
            y_high[c, into, :] = out[c, pl.ds(geo.sy + plane, geo.X, stride=geo.Y), :]
        at = 2 * geo.X
        for buffer in (y_low, y_high):
            buffer[c, at : at + 1, :] = rows[c : c + 1]
            buffer[c, at + 1 : at + 2, :] = rows[4 + c : 5 + c]


def sum_done(geo, flags, face, rows_in, from_low, from_high, wide, total):
    has_low, has_high = flags[2], flags[3]
    at = 2 * geo.X
    rows = add_rows_y(
        geo, rows_in[...], slab_rows(from_low, at), slab_rows(from_high, at), has_low, has_high
    )
    wide[...] = jnp.zeros_like(wide)
    for c in range(3):
        wide[: geo.RP, :] = face[c]
        for plane in range(2):
            part = slice(plane * geo.X, (plane + 1) * geo.X)
            low_at = pl.ds(plane, geo.X, stride=geo.Y)
            high_at = pl.ds(geo.sy + plane, geo.X, stride=geo.Y)
            wide[low_at, :] = wide[low_at, :] + jnp.where(has_low, from_low[c, part, :], 0.0)
            wide[high_at, :] = wide[high_at, :] + jnp.where(has_high, from_high[c, part, :], 0.0)
        total[c, 0:8, :] = jnp.zeros((8, geo.LP), F32)
        total[c, geo.ZR - 8 : geo.ZR, :] = jnp.zeros((8, geo.LP), F32)
        total[c, 2 : 2 + geo.sz, :] = wide[...].T
        total[c, 1:2, :] = rows[c : c + 1]
        total[c, geo.sz + 2 : geo.sz + 3, :] = rows[4 + c : 5 + c]


def update(geo, total, u, u_old, jinv, new_u, norm):
    lane, x, y = lane_xy(geo, (8, geo.LP))
    owned = (x >= 1) & (x <= geo.sx) & (y >= 1) & (y <= geo.sy)
    squares = jnp.zeros((8, geo.LP), F32)
    for k in range(geo.ZR // 8):
        rows = slice(8 * k, 8 * k + 8)
        now = [u[c, rows, :] for c in range(3)]
        residual = [now[c] - u_old[c, rows, :] - step_size * total[c, rows, :] for c in range(3)]
        for r in range(3):
            applied = sum(jinv[3 * r + m, rows, :] * residual[m] for m in range(3))
            new_u[r, rows, :] = now[r] - applied
        z = lax.broadcasted_iota(jnp.int32, (8, geo.LP), 0) + (8 * k - 1)
        mask = owned & (z >= 1) & (z <= geo.sz)
        square = residual[0] * residual[0] + residual[1] * residual[1] + residual[2] * residual[2]
        squares = squares + jnp.where(mask, square, 0.0)
    norm[...] = squares


def steps(code):
    which = code >> 1
    direction = 1 - 2 * (code & 1)
    return [jnp.where(which == k, direction, 0) for k in range(3)]


def split(value):
    high = value.astype(BF16).astype(F32)
    return high, value - high


class Codes:
    def __init__(self, geo, codes, rows):
        Y = 8
        inside, along, offset, across = [codes[k, rows, :] for k in range(4)]
        self.e1, self.e3 = e1, e3 = steps(along), steps(across)
        third = (offset * 43) >> 7
        ninth = (offset * 57) >> 9
        self.shift = shift = [ninth - 1, third - 3 * ninth - 1, offset - 3 * third - 1]
        lane_a = ((inside >> 5) + 2) * Y + ((inside >> 3) & 3) + 2
        depth_a = (inside & 7) + 2
        lane_b = lane_a + e1[0] * Y + e1[1]
        depth_b = depth_a + e1[2]
        lane_c = lane_a + shift[0] * Y + shift[1]
        depth_c = depth_a + shift[2]
        lane_d = lane_c + e3[0] * Y + e3[1]
        depth_d = depth_c + e3[2]
        self.lane4 = jnp.concatenate([lane_a, lane_b, lane_c, lane_d], 1)
        self.depth4 = jnp.concatenate([depth_a, depth_b, depth_c, depth_d], 1)


def group_rows(turn):
    if isinstance(turn, int):
        return slice(turn * GROUP, (turn + 1) * GROUP)
    return pl.ds(pl.multiple_of(turn * GROUP, GROUP), GROUP)


def hot_kernel(geo, codes, hots):
    depth = lax.broadcasted_iota(jnp.int32, (16, 512), 0).astype(jnp.int16)
    one, zero = jnp.ones((16, 512), BF16), jnp.zeros((16, 512), BF16)

    def one_group(turn, carry):
        lane4 = Codes(geo, codes, group_rows(turn)).lane4
        for t in range(GROUP):
            lanes = jnp.broadcast_to(lane4[t : t + 1], (16, 512)).astype(jnp.int16)
            for k in range(WINDOW // 16):
                hit = (lanes - jnp.int16(16 * k)) == depth
                hots[turn * GROUP + t, 16 * k : 16 * k + 16, :] = jnp.where(hit, one, zero)
        return carry

    lax.fori_loop(0, hots.shape[0] // GROUP, one_group, 0)


def pair_pass(geo, base, u, hots, codes, groups, both, work, frozen, force):
    windows, pieces, sums, lanes, anchors, arrived = work
    fetch = pltpu.make_async_copy(base, anchors, arrived)
    LP, ZR = geo.LP, geo.ZR
    planes = geo.bx * geo.by
    kinds = (0, 1) if both else (0,)
    gates = window_gates(geo)
    whole = u[...].reshape(3 * ZR, LP)
    high = whole.astype(BF16)
    low = (whole - high.astype(F32)).astype(BF16)
    for plane in range(planes):
        gate = gates[:, WINDOW * plane : WINDOW * (plane + 1)]
        zero = jnp.zeros_like(gate)
        gate = jnp.concatenate(
            [jnp.concatenate([gate, zero], 1), jnp.concatenate([zero, gate], 1)], 0
        ).astype(BF16)
        lanes[0] = jnp.dot(jnp.concatenate([high, low], 1), gate, preferred_element_type=F32)
        for k in range(geo.bz):
            for c in range(3):
                rows = slice(ZR * c + 8 * k, ZR * c + 8 * k + 16)
                windows[geo.bz * plane + k, 16 * c : 16 * c + 16, :] = lanes[0, rows, :].astype(BF16)
    sums[...] = jnp.zeros_like(sums)
    depths = lax.broadcasted_iota(jnp.int32, (16, 512), 0)
    def place_of(turn, t):
        return anchors[turn * GROUP + t]

    sub = lax.broadcasted_iota(jnp.int32, (8, 128), 0)
    even = [(sub & step) == 0 for step in (1, 2, 4)]

    def merged(low, high, level):
        keep, step = even[level], 1 << level
        moved = pltpu.roll(jnp.where(keep, high, low), 8 - step, 0)
        return jnp.where(keep, low, high) + moved

    def gather_tile(turn, t, depth4):
        hot = hots[turn * GROUP + t]
        picked = jnp.dot(
            windows[place_of(turn, t)],
            jnp.concatenate([hot, hot], 0),
            preferred_element_type=F32,
        )
        mask = depths == depth4[t : t + 1]
        parts = []
        for c in range(3):
            part = jnp.where(mask, picked[16 * c : 16 * c + 16], 0.0)
            part = part[:8] + part[8:]
            parts += [part[:, 128 * n : 128 * n + 128] for n in range(4)]
        return parts

    def scatter_tile(turn, t, depth4, slot):
        mask = depths == depth4[t : t + 1]
        spread = jnp.concatenate(
            [
                jnp.where(mask, pieces[slot, k, t : t + 1, :], 0.0).astype(BF16)
                for k in range(6 * len(kinds))
            ],
            0,
        )
        pushed = lax.dot_general(
            spread, hots[turn * GROUP + t], (((1,), (1,)), ((), ())), preferred_element_type=F32
        )
        place = place_of(turn, t)
        for group in kinds:
            part = pushed[96 * group : 96 * group + 48] + pushed[96 * group + 48 : 96 * group + 96]
            sums[group, place] += part

    def pair_forces(turn, code, points, slot):
        kind = groups[group_rows(turn), :]
        line_one, line_two, apart = [], [], []
        for c in range(3):
            ua, ub, uc, ud = points[4 * c : 4 * c + 4]
            step1, step3 = code.e1[c].astype(F32), code.e3[c].astype(F32)
            line_one.append((ub - ua) + step1)
            line_two.append((ud - uc) + step3)
            lattice = code.shift[c].astype(F32) + 0.5 * (step3 - step1)
            apart.append(0.5 * ((uc + ud) - (ua + ub)) + lattice)
        square = apart[0] * apart[0] + apart[1] * apart[1] + apart[2] * apart[2] + core_square
        product = (
            line_one[0] * line_two[0] + line_one[1] * line_two[1] + line_one[2] * line_two[2]
        )
        coupling = (0.5 * stiffness) * product / (square * jnp.sqrt(square))
        at = 0
        for group in kinds:
            chosen = jnp.where(kind == group, coupling, 0.0)
            halves = [split(chosen * apart[c]) for c in range(3)]
            for piece in range(2):
                for c in range(3):
                    h = halves[c][piece]
                    pieces[slot, at] = jnp.concatenate([-h, -h, h, h], 1)
                    at += 1

    def one_group(turn, do_scatter, do_gather):
        before = Codes(geo, codes, group_rows(turn - 1)) if do_scatter else None
        code = Codes(geo, codes, group_rows(turn)) if do_gather else None
        waiting = []
        ahead = AHEAD if do_gather and do_scatter else 0
        for t in range(GROUP + ahead):
            if do_gather and t >= ahead:
                one = t - ahead
                parts, level = gather_tile(turn, one, code.depth4), 0
                while (one >> level) & 1:
                    parts = [merged(x, y, level) for x, y in zip(waiting.pop(), parts)]
                    level += 1
                waiting.append(parts)
            if do_scatter and t < GROUP:
                scatter_tile(turn - 1, t, before.depth4, (turn - 1) & 1)
        if do_gather:
            pair_forces(turn, code, waiting.pop(), turn & 1)

    def looped(turn, carry):
        one_group(turn, True, True)
        return carry

    count = geo.tiles // GROUP
    fetch.wait()
    one_group(0, False, True)
    lax.fori_loop(1, count, looped, 0)
    one_group(count, True, False)

    gates = gates.astype(BF16)

    def folded(group):
        for c in range(3):
            for k in range(geo.bz + 1):
                parts = []
                for plane in range(planes):
                    rows = jnp.zeros((8, WINDOW), F32)
                    at = geo.bz * plane + k
                    if k < geo.bz:
                        rows = rows + sums[group, at, 16 * c : 16 * c + 8, :]
                    if k > 0:
                        rows = rows + sums[group, at - 1, 16 * c + 8 : 16 * c + 16, :]
                    parts.append(rows)
                rows = slice(ZR * c + 8 * k, ZR * c + 8 * k + 8)
                for pair in range(0, planes, 2):
                    lanes[pair // 2, rows, :] = jnp.concatenate(parts[pair : pair + 2], 1)
        value = jnp.zeros((3 * ZR, LP), F32)
        for pair in range(planes // 2):
            gate = gates[:, 128 * pair : 128 * pair + 128]
            for piece in split(lanes[pair]):
                value = value + lax.dot_general(
                    piece.astype(BF16), gate, (((1,), (1,)), ((), ())), preferred_element_type=F32
                )
        return value.reshape(3, ZR, LP)

    if both:
        frozen[...] = folded(1)
    force[...] = folded(0) + frozen[...]


def window_gates(geo):
    shape = (geo.LP, WINDOW * geo.bx * geo.by)
    lane = lax.broadcasted_iota(jnp.int32, shape, 0)
    column = lax.broadcasted_iota(jnp.int32, shape, 1)
    plane, cell = column // WINDOW, column % WINDOW
    x = 4 * (plane // geo.by) - 1 + cell // 8
    y = 4 * (plane % geo.by) - 1 + cell % 8
    inside = (x >= 0) & (x < geo.X) & (y >= 0) & (y < geo.Y)
    return jnp.where(inside & (lane == x * geo.Y + y), 1.0, 0.0)


def start_fetch(base, work):
    pltpu.make_async_copy(base, work[4], work[5]).start()


def first_kernel(
    geo, bases, face, rows_in, from_low, from_high, hots, codes, groups,
    u, u_old, jinv, frozen, force, zbuf, wide, *work,
):
    start_fetch(bases, work)
    targets = [u.at[c] for c in range(3)] + [u_old.at[c] for c in range(3)]
    targets = targets + [jinv.at[c] for c in range(9)]
    fill_done(geo, edges(), face, rows_in, from_low, from_high, wide, targets)
    pair_pass(geo, bases, u, hots, codes, groups, True, work, frozen, force)
    z_slab(geo, force, zbuf)


def next_kernel(
    geo, bases, face, rows_in, from_low, from_high, u, u_old, jinv, frozen, hots, codes, groups,
    new_u, norm, force, zbuf, wide, total, *work,
):
    start_fetch(bases, work)
    sum_done(geo, edges(), face, rows_in, from_low, from_high, wide, total)
    update(geo, total, u, u_old, jinv, new_u, norm)
    pair_pass(geo, bases, new_u, hots, codes, groups, False, work, frozen, force)
    z_slab(geo, force, zbuf)


def last_kernel(
    geo, face, rows_in, from_low, from_high, u, u_old, jinv, norm_0, norm_1,
    out, norms, wide, total, new_u, norm_2,
):
    sum_done(geo, edges(), face, rows_in, from_low, from_high, wide, total)
    update(geo, total, u, u_old, jinv, new_u, norm_2)
    for c in range(3):
        wide[...] = new_u[c, 2 : 2 + geo.sz, :].T
        for x in range(geo.sx):
            start = (x + 1) * geo.Y + 1
            out[c, x * geo.sy : (x + 1) * geo.sy, :] = wide[start : start + geo.sy, :]
    lane = lax.broadcasted_iota(jnp.int32, (1, geo.LP), 1)
    line = jnp.zeros((1, geo.LP), F32)
    for k, norm in enumerate((norm_0, norm_1, norm_2)):
        line = line + jnp.where(lane == k, jnp.sum(norm[...]), 0.0)
    norms[...] = jnp.broadcast_to(line, norms.shape)


def ring(shard, axis, by):
    count = lax.axis_size(axis)
    return lax.ppermute(shard, axis, [(i, (i + by) % count) for i in range(count)])


def swap(low_buffer, high_buffer, axis):
    return ring(high_buffer, axis, 1), ring(low_buffer, axis, -1)


def swap_joint(buffer, axis):
    if lax.axis_size(axis) <= 2:
        other = ring(buffer, axis, 1)
        return other, other
    return ring(buffer, axis, 1), ring(buffer, axis, -1)


def per_device(u_old, u_trial, jacobian_inverse, tile_base, pair_codes, pair_groups):
    sx, sy, sz = u_old.shape[1:]
    geo = Geo(sx, sy, sz, tile_base.shape[0])
    if sz != 128 or geo.LP != 128 or sy % 8 or geo.bx % 2 or geo.tiles % GROUP:
        raise ValueError("unsupported sizes")
    axes = ("gx", "gy", "gz")
    cells = 3.0 * sx * sy * sz
    devices = 1
    for axis in axes:
        devices = devices * lax.axis_size(axis)
    cells = cells * devices
    vmem, anywhere = pl.BlockSpec(memory_space=pltpu.VMEM), pl.BlockSpec(memory_space=pl.ANY)

    def arr(*shape):
        return jax.ShapeDtypeStruct(shape, F32)

    def call(kernel, name, bases, operands, outs, scratch=(), cost=None, flags=None):
        return pl.pallas_call(
            functools.partial(kernel, geo),
            out_shape=outs,
            in_specs=[anywhere] * len(bases) + [vmem] * len(operands),
            out_specs=[vmem] * len(outs),
            scratch_shapes=list(scratch),
            compiler_params=pltpu.CompilerParams(vmem_limit_bytes=VMEM_GRANT, flags=flags),
            cost_estimate=cost,
            name=name,
        )(*bases, *operands)

    def spot(*shape, dtype=F32):
        return pltpu.VMEM(shape, dtype)

    anchors = geo.bx * geo.by * geo.bz

    def work(count):
        return [
            spot(anchors, 48, 2 * WINDOW, dtype=BF16),
            spot(2, 6 * count, GROUP, 512),
            spot(count, anchors, 48, WINDOW),
            spot(geo.bx * geo.by // 2, 3 * geo.ZR, geo.LP),
            pltpu.SMEM((geo.tiles,), jnp.int32),
            pltpu.SemaphoreType.DMA(()),
        ]

    square = spot(geo.LP, sz)
    lattice = arr(3, geo.ZR, geo.LP)
    faces3, rows8, zshape = arr(3, geo.RP, sz), arr(8, geo.LP), arr(3, 8, geo.LP)
    slab = arr(3, geo.slab, 128)

    ut = u_trial.reshape(3, sx * sy, sz)
    uo = u_old.reshape(3, sx * sy, sz)
    ji = jacobian_inverse.reshape(9, sx * sy, sz)

    hots = call(
        hot_kernel,
        "hots",
        [],
        [pair_codes],
        [jax.ShapeDtypeStruct((geo.tiles, WINDOW, 512), BF16)],
        cost=pl.CostEstimate(flops=0, bytes_accessed=16 << 20, transcendentals=0),
    )[0]
    part_x = arr(15 * sy, 128)
    face, zbuf, x_low, x_high = call(
        fill_z_kernel,
        "fill_z",
        [],
        [jnp.concatenate([ut, uo, ji], 0)],
        [arr(15, geo.RP, sz), arr(32, geo.LP), part_x, part_x],
        [square],
    )
    z_low, z_high = swap_joint(zbuf, "gz")
    wide_x = arr(15 * sy + 32, 128)
    x_low, x_high = call(
        fill_x_kernel, "fill_x", [], [x_low, x_high, z_low, z_high], [wide_x, wide_x]
    )
    from_low, from_high = swap(x_low, x_high, "gx")
    wide_y = arr(fill_y_rows(geo), 128)
    face, rows, y_low, y_high = call(
        fill_y_kernel,
        "fill_y",
        [],
        [face, z_low, z_high, from_low, from_high],
        [arr(15, geo.RP, sz), arr(32, geo.LP), wide_y, wide_y],
    )
    from_low, from_high = swap(y_low, y_high, "gy")
    u, uo_l, ji_l, frozen, force, zbuf = call(
        first_kernel,
        "first_pass",
        [tile_base],
        [face, rows, from_low, from_high, hots, pair_codes, pair_groups],
        [lattice, lattice, arr(9, geo.ZR, geo.LP), lattice, lattice, zshape],
        [square] + work(2),
    )

    norm_list = []
    for iteration in range(ITERS):
        z_low, z_high = swap_joint(zbuf, "gz")
        face, rows, x_low, x_high = call(
            sum_x_kernel, "sum_x", [], [force, z_low, z_high], [faces3, rows8, slab, slab]
        )
        from_low, from_high = swap(x_low, x_high, "gx")
        face, rows, y_low, y_high = call(
            sum_y_kernel,
            "sum_y",
            [],
            [face, rows, from_low, from_high],
            [faces3, rows8, slab, slab],
        )
        from_low, from_high = swap(y_low, y_high, "gy")
        total = spot(3, geo.ZR, geo.LP)
        if iteration < ITERS - 1:
            u, norm, force, zbuf = call(
                next_kernel,
                "next_pass",
                [tile_base],
                [face, rows, from_low, from_high, u, uo_l, ji_l, frozen, hots, pair_codes, pair_groups],
                [lattice, rows8, lattice, zshape],
                [square, total] + work(1),
            )
            norm_list.append(norm)
    out, norms = call(
        last_kernel,
        "last",
        [],
        [face, rows, from_low, from_high, u, uo_l, ji_l] + norm_list,
        [arr(3, sx * sy, sz), arr(devices, 128)],
        [square, spot(3, geo.ZR, geo.LP), spot(3, geo.ZR, geo.LP), spot(8, geo.LP)],
    )
    spread = lax.all_to_all(norms.reshape(devices, 1, 128), axes, 0, 0)
    squares = jnp.sum(spread, axis=(0, 1))[:ITERS]
    return out.reshape(3, sx, sy, sz), jnp.sqrt(squares / cells)


def solution(mesh):
    return jax.shard_map(
        per_device,
        mesh=mesh,
        in_specs=(
            P(None, "gx", "gy", "gz"),
            P(None, "gx", "gy", "gz"),
            P(None, None, "gx", "gy", "gz"),
            P(("gx", "gy", "gz")),
            P(None, ("gx", "gy", "gz"), None),
            P(("gx", "gy", "gz"), None),
        ),
        out_specs=(P(None, "gx", "gy", "gz"), P()),
        check_vma=False,
    )
```

```python
import functools

import jax
import jax.numpy as jnp
from jax import lax
from jax.experimental import pallas as pl
from jax.experimental.pallas import tpu as pltpu
from jax.sharding import PartitionSpec as P

ITERS = 3
step_size = 0.5
stiffness = 0.5
core_square = 0.5

F32 = jnp.float32
BF16 = jnp.bfloat16
GROUP = 8
WINDOW = 64
AHEAD = 0
VMEM_GRANT = 12 << 20


class Geo:
    def __init__(self, sx, sy, sz, tiles):
        self.sx, self.sy, self.sz, self.tiles = sx, sy, sz, tiles
        self.X, self.Y = sx + 2, sy + 2
        self.XY = self.X * self.Y
        self.LP = -(-self.XY // 128) * 128
        self.RP = -(-self.XY // 8) * 8
        self.ZR = sz + 8
        self.bx = sx // 4
        self.by = sy // 4
        self.bz = sz // 8
        self.slab = -(-(2 * max(self.X, self.Y) + 2) // 8) * 8


def edges():
    found = []
    for axis in ("gx", "gy", "gz"):
        at = lax.axis_index(axis)
        found += [at > 0, at < lax.axis_size(axis) - 1]
    return found


def roll(x, shift, size):
    return pltpu.roll(x, shift % size, 1)


def lane_xy(geo, shape):
    lane = lax.broadcasted_iota(jnp.int32, shape, len(shape) - 1)
    x = jnp.zeros_like(lane)
    for k in range(1, geo.X):
        x = x + (lane >= k * geo.Y).astype(jnp.int32)
    return lane, x, lane - x * geo.Y


def add_rows_x(geo, rows, low, high, has_low, has_high):
    lane, _, _ = lane_xy(geo, rows.shape)
    span = geo.sx * geo.Y
    from_low = roll(low, -span, geo.LP)
    from_high = roll(high, span, geo.LP)
    rows = rows + jnp.where((lane < 2 * geo.Y) & has_low, from_low, 0.0)
    return rows + jnp.where((lane >= span) & (lane < geo.XY) & has_high, from_high, 0.0)


def add_rows_y(geo, rows, low, high, has_low, has_high):
    lane, _, y = lane_xy(geo, rows.shape)
    from_low = roll(low, -geo.sy, geo.LP)
    from_high = roll(high, geo.sy, geo.LP)
    inside = lane < geo.XY
    rows = rows + jnp.where((y < 2) & inside & has_low, from_low, 0.0)
    return rows + jnp.where((y >= geo.sy) & inside & has_high, from_high, 0.0)


def fill_z_kernel(geo, mine, face, zbuf, x_low, x_high, wide):
    wide[...] = jnp.zeros_like(wide)
    zbuf[...] = jnp.zeros_like(zbuf)
    last = (geo.sx - 1) * geo.sy
    for c in range(15):
        for x in range(geo.sx):
            start = (x + 1) * geo.Y + 1
            wide[start : start + geo.sy, :] = mine[c, x * geo.sy : (x + 1) * geo.sy, :]
        x_low[c * geo.sy : (c + 1) * geo.sy, :] = mine[c, 0 : geo.sy, :]
        x_high[c * geo.sy : (c + 1) * geo.sy, :] = mine[c, last : last + geo.sy, :]
        value = wide[...]
        face[c] = value[: geo.RP]
        turned = value.T
        zbuf[c : c + 1, :] = turned[0:1]
        zbuf[16 + c : 17 + c, :] = turned[geo.sz - 1 : geo.sz]


def fill_rows(flags, z_low, z_high):
    low = jnp.where(flags[4], z_low[16:32, :], 0.0)
    high = jnp.where(flags[5], z_high[0:16, :], 0.0)
    return jnp.concatenate([low, high], 0)


def fill_x_kernel(geo, low, high, z_low, z_high, x_low, x_high):
    rows = fill_rows(edges(), z_low, z_high)
    count = 15 * geo.sy
    x_low[:count, :] = low[...]
    x_high[:count, :] = high[...]
    x_low[count : count + 32, :] = rows
    x_high[count : count + 32, :] = rows


def fill_y_kernel(geo, face, z_low, z_high, from_low, from_high, out, rows_out, y_low, y_high):
    flags = edges()
    has_low, has_high = flags[0], flags[1]
    count = 15 * geo.sy
    rows = add_rows_x(
        geo,
        fill_rows(flags, z_low, z_high),
        from_low[count : count + 32, :],
        from_high[count : count + 32, :],
        has_low,
        has_high,
    )
    rows_out[...] = rows
    out[...] = face[...]
    y_low[...] = jnp.zeros_like(y_low)
    y_high[...] = jnp.zeros_like(y_high)
    top = (geo.sx + 1) * geo.Y + 1
    for c in range(15):
        part = slice(c * geo.sy, (c + 1) * geo.sy)
        out[c, 1 : 1 + geo.sy, :] = jnp.where(has_low, from_low[part, :], 0.0)
        out[c, top : top + geo.sy, :] = jnp.where(has_high, from_high[part, :], 0.0)
        into = slice(c * geo.X, (c + 1) * geo.X)
        y_low[into, :] = out[c, pl.ds(1, geo.X, stride=geo.Y), :]
        y_high[into, :] = out[c, pl.ds(geo.sy, geo.X, stride=geo.Y), :]
    tail = fill_y_rows(geo) - 32
    y_low[tail : tail + 32, :] = rows
    y_high[tail : tail + 32, :] = rows


def fill_y_rows(geo):
    return -(-15 * geo.X // 8) * 8 + 32


def fill_done(geo, flags, face, rows_in, from_low, from_high, wide, targets):
    has_low, has_high = flags[2], flags[3]
    tail = fill_y_rows(geo) - 32
    rows = add_rows_y(
        geo,
        rows_in[...],
        from_low[tail : tail + 32, :],
        from_high[tail : tail + 32, :],
        has_low,
        has_high,
    )
    wide[...] = jnp.zeros_like(wide)
    for c, target in enumerate(targets):
        wide[: geo.RP, :] = face[c]
        part = slice(c * geo.X, (c + 1) * geo.X)
        wide[pl.ds(0, geo.X, stride=geo.Y), :] = jnp.where(has_low, from_low[part, :], 0.0)
        wide[pl.ds(geo.sy + 1, geo.X, stride=geo.Y), :] = jnp.where(has_high, from_high[part, :], 0.0)
        target[0:8, :] = jnp.zeros((8, geo.LP), F32)
        target[geo.ZR - 8 : geo.ZR, :] = jnp.zeros((8, geo.LP), F32)
        target[2 : 2 + geo.sz, :] = wide[...].T
        target[1:2, :] = rows[c : c + 1]
        target[geo.sz + 2 : geo.sz + 3, :] = rows[16 + c : 17 + c]


def z_slab(geo, force, zbuf):
    zbuf[...] = jnp.zeros_like(zbuf)
    for c in range(3):
        zbuf[c, 0:2, :] = force[c, 1:3, :]
        zbuf[c, 2:4, :] = force[c, geo.sz + 1 : geo.sz + 3, :]


def sum_x_kernel(geo, force, z_low, z_high, face, rows_out, x_low, x_high):
    flags = edges()
    has_low, has_high = flags[4], flags[5]
    rows_out[...] = jnp.zeros_like(rows_out)
    x_low[...] = jnp.zeros_like(x_low)
    x_high[...] = jnp.zeros_like(x_high)
    span, two = geo.sx * geo.Y, 2 * geo.Y
    row = lax.broadcasted_iota(jnp.int32, (geo.sz, geo.LP), 0)
    for c in range(3):
        low = jnp.where(has_low, z_low[c, 2:4, :], 0.0)
        high = jnp.where(has_high, z_high[c, 0:2, :], 0.0)
        value = force[c, 2 : 2 + geo.sz, :]
        value = value + jnp.where(row == 0, low[1:2], 0.0)
        value = value + jnp.where(row == geo.sz - 1, high[0:1], 0.0)
        turned = value.T[: geo.RP]
        face[c] = turned
        low_row = force[c, 1:2, :] + low[0:1]
        high_row = force[c, geo.sz + 2 : geo.sz + 3, :] + high[1:2]
        rows_out[c : c + 1, :] = low_row
        rows_out[4 + c : 5 + c, :] = high_row
        x_low[c, 0:two, :] = face[c, 0:two, :]
        x_high[c, 0:two, :] = face[c, span : span + two, :]
        for buffer in (x_low, x_high):
            buffer[c, two : two + 1, :] = low_row
            buffer[c, two + 1 : two + 2, :] = high_row


def slab_rows(buffer, at):
    zero = jnp.zeros_like(buffer[0, at : at + 1, :])
    low = [buffer[c, at : at + 1, :] for c in range(3)]
    high = [buffer[c, at + 1 : at + 2, :] for c in range(3)]
    return jnp.concatenate(low + [zero] + high + [zero], 0)


def sum_y_kernel(geo, face, rows_in, from_low, from_high, out, rows_out, y_low, y_high):
    flags = edges()
    has_low, has_high = flags[0], flags[1]
    span, two = geo.sx * geo.Y, 2 * geo.Y
    rows = add_rows_x(
        geo, rows_in[...], slab_rows(from_low, two), slab_rows(from_high, two), has_low, has_high
    )
    rows_out[...] = rows
    out[...] = face[...]
    y_low[...] = jnp.zeros_like(y_low)
    y_high[...] = jnp.zeros_like(y_high)
    for c in range(3):
        out[c, 0:two, :] += jnp.where(has_low, from_low[c, 0:two, :], 0.0)
        out[c, span : span + two, :] += jnp.where(has_high, from_high[c, 0:two, :], 0.0)
        for plane in range(2):
            into = slice(plane * geo.X, (plane + 1) * geo.X)
            y_low[c, into, :] = out[c, pl.ds(plane, geo.X, stride=geo.Y), :]
            y_high[c, into, :] = out[c, pl.ds(geo.sy + plane, geo.X, stride=geo.Y), :]
        at = 2 * geo.X
        for buffer in (y_low, y_high):
            buffer[c, at : at + 1, :] = rows[c : c + 1]
            buffer[c, at + 1 : at + 2, :] = rows[4 + c : 5 + c]


def sum_done(geo, flags, face, rows_in, from_low, from_high, wide, total):
    has_low, has_high = flags[2], flags[3]
    at = 2 * geo.X
    rows = add_rows_y(
        geo, rows_in[...], slab_rows(from_low, at), slab_rows(from_high, at), has_low, has_high
    )
    wide[...] = jnp.zeros_like(wide)
    for c in range(3):
        wide[: geo.RP, :] = face[c]
        for plane in range(2):
            part = slice(plane * geo.X, (plane + 1) * geo.X)
            low_at = pl.ds(plane, geo.X, stride=geo.Y)
            high_at = pl.ds(geo.sy + plane, geo.X, stride=geo.Y)
            wide[low_at, :] = wide[low_at, :] + jnp.where(has_low, from_low[c, part, :], 0.0)
            wide[high_at, :] = wide[high_at, :] + jnp.where(has_high, from_high[c, part, :], 0.0)
        total[c, 0:8, :] = jnp.zeros((8, geo.LP), F32)
        total[c, geo.ZR - 8 : geo.ZR, :] = jnp.zeros((8, geo.LP), F32)
        total[c, 2 : 2 + geo.sz, :] = wide[...].T
        total[c, 1:2, :] = rows[c : c + 1]
        total[c, geo.sz + 2 : geo.sz + 3, :] = rows[4 + c : 5 + c]


def update(geo, total, u, u_old, jinv, new_u, norm):
    lane, x, y = lane_xy(geo, (8, geo.LP))
    owned = (x >= 1) & (x <= geo.sx) & (y >= 1) & (y <= geo.sy)
    squares = jnp.zeros((8, geo.LP), F32)
    for k in range(geo.ZR // 8):
        rows = slice(8 * k, 8 * k + 8)
        now = [u[c, rows, :] for c in range(3)]
        residual = [now[c] - u_old[c, rows, :] - step_size * total[c, rows, :] for c in range(3)]
        for r in range(3):
            applied = sum(jinv[3 * r + m, rows, :] * residual[m] for m in range(3))
            new_u[r, rows, :] = now[r] - applied
        z = lax.broadcasted_iota(jnp.int32, (8, geo.LP), 0) + (8 * k - 1)
        mask = owned & (z >= 1) & (z <= geo.sz)
        square = residual[0] * residual[0] + residual[1] * residual[1] + residual[2] * residual[2]
        squares = squares + jnp.where(mask, square, 0.0)
    norm[...] = squares


def steps(code):
    which = code >> 1
    direction = 1 - 2 * (code & 1)
    return [jnp.where(which == k, direction, 0) for k in range(3)]


def split(value):
    high = value.astype(BF16).astype(F32)
    return high, value - high


class Codes:
    def __init__(self, geo, codes, rows):
        Y = 8
        inside, along, offset, across = [codes[k, rows, :] for k in range(4)]
        self.e1, self.e3 = e1, e3 = steps(along), steps(across)
        third = (offset * 43) >> 7
        ninth = (offset * 57) >> 9
        self.shift = shift = [ninth - 1, third - 3 * ninth - 1, offset - 3 * third - 1]
        lane_a = ((inside >> 5) + 2) * Y + ((inside >> 3) & 3) + 2
        depth_a = (inside & 7) + 2
        lane_b = lane_a + e1[0] * Y + e1[1]
        depth_b = depth_a + e1[2]
        lane_c = lane_a + shift[0] * Y + shift[1]
        depth_c = depth_a + shift[2]
        lane_d = lane_c + e3[0] * Y + e3[1]
        depth_d = depth_c + e3[2]
        self.lane4 = jnp.concatenate([lane_a, lane_b, lane_c, lane_d], 1)
        self.depth4 = jnp.concatenate([depth_a, depth_b, depth_c, depth_d], 1)


def group_rows(turn):
    if isinstance(turn, int):
        return slice(turn * GROUP, (turn + 1) * GROUP)
    return pl.ds(pl.multiple_of(turn * GROUP, GROUP), GROUP)


def hot_kernel(geo, codes, hots):
    depth = lax.broadcasted_iota(jnp.int32, (16, 512), 0).astype(jnp.int16)
    one, zero = jnp.ones((16, 512), BF16), jnp.zeros((16, 512), BF16)

    def one_group(turn, carry):
        lane4 = Codes(geo, codes, group_rows(turn)).lane4
        for t in range(GROUP):
            lanes = jnp.broadcast_to(lane4[t : t + 1], (16, 512)).astype(jnp.int16)
            for k in range(WINDOW // 16):
                hit = (lanes - jnp.int16(16 * k)) == depth
                hots[turn * GROUP + t, 16 * k : 16 * k + 16, :] = jnp.where(hit, one, zero)
        return carry

    lax.fori_loop(0, hots.shape[0] // GROUP, one_group, 0)


def pair_pass(geo, base, u, hots, codes, groups, both, work, frozen, force):
    windows, pieces, sums, lanes, anchors, arrived = work
    fetch = pltpu.make_async_copy(base, anchors, arrived)
    LP, ZR = geo.LP, geo.ZR
    planes = geo.bx * geo.by
    kinds = (0, 1) if both else (0,)
    gates = window_gates(geo)
    whole = u[...].reshape(3 * ZR, LP)
    high = whole.astype(BF16)
    low = (whole - high.astype(F32)).astype(BF16)
    both_pieces = jnp.concatenate([high, low], 1)
    for pair in range(0, planes, 2):
        blocks = []
        for plane in (pair, pair + 1):
            gate = gates[:, WINDOW * plane : WINDOW * (plane + 1)]
            zero = jnp.zeros_like(gate)
            blocks.append(
                jnp.concatenate(
                    [jnp.concatenate([gate, zero], 1), jnp.concatenate([zero, gate], 1)], 0
                )
            )
        wanted = jnp.concatenate(blocks, 1).astype(BF16)
        found = jnp.dot(both_pieces, wanted, preferred_element_type=F32)
        for j in range(2):
            lanes[j] = found[:, 128 * j : 128 * j + 128]
            for k in range(geo.bz):
                for c in range(3):
                    rows = slice(ZR * c + 8 * k, ZR * c + 8 * k + 16)
                    at = geo.bz * (pair + j) + k
                    windows[at, 16 * c : 16 * c + 16, :] = lanes[j, rows, :].astype(BF16)
    sums[...] = jnp.zeros_like(sums)
    depths = lax.broadcasted_iota(jnp.int32, (16, 512), 0)
    def place_of(turn, t):
        return anchors[turn * GROUP + t]

    sub = lax.broadcasted_iota(jnp.int32, (8, 128), 0)
    even = [(sub & step) == 0 for step in (1, 2, 4)]

    def merged(low, high, level):
        keep, step = even[level], 1 << level
        moved = pltpu.roll(jnp.where(keep, high, low), 8 - step, 0)
        return jnp.where(keep, low, high) + moved

    def gather_tile(turn, t, depth4):
        hot = hots[turn * GROUP + t]
        picked = jnp.dot(
            windows[place_of(turn, t)],
            jnp.concatenate([hot, hot], 0),
            preferred_element_type=F32,
        )
        mask = depths == depth4[t : t + 1]
        parts = []
        for c in range(3):
            part = jnp.where(mask, picked[16 * c : 16 * c + 16], 0.0)
            part = part[:8] + part[8:]
            parts += [part[:, 128 * n : 128 * n + 128] for n in range(4)]
        return parts

    def scatter_tile(turn, t, depth4, slot):
        mask = depths == depth4[t : t + 1]
        spread = jnp.concatenate(
            [
                jnp.where(mask, pieces[slot, k, t : t + 1, :], 0.0).astype(BF16)
                for k in range(6 * len(kinds))
            ],
            0,
        )
        pushed = lax.dot_general(
            spread, hots[turn * GROUP + t], (((1,), (1,)), ((), ())), preferred_element_type=F32
        )
        place = place_of(turn, t)
        for group in kinds:
            part = pushed[96 * group : 96 * group + 48] + pushed[96 * group + 48 : 96 * group + 96]
            sums[group, place] += part

    def pair_forces(turn, code, points, slot):
        kind = groups[group_rows(turn), :]
        line_one, line_two, apart = [], [], []
        for c in range(3):
            ua, ub, uc, ud = points[4 * c : 4 * c + 4]
            step1, step3 = code.e1[c].astype(F32), code.e3[c].astype(F32)
            line_one.append((ub - ua) + step1)
            line_two.append((ud - uc) + step3)
            lattice = code.shift[c].astype(F32) + 0.5 * (step3 - step1)
            apart.append(0.5 * ((uc + ud) - (ua + ub)) + lattice)
        square = apart[0] * apart[0] + apart[1] * apart[1] + apart[2] * apart[2] + core_square
        product = (
            line_one[0] * line_two[0] + line_one[1] * line_two[1] + line_one[2] * line_two[2]
        )
        coupling = (0.5 * stiffness) * product / (square * jnp.sqrt(square))
        at = 0
        for group in kinds:
            chosen = jnp.where(kind == group, coupling, 0.0)
            halves = [split(chosen * apart[c]) for c in range(3)]
            for piece in range(2):
                for c in range(3):
                    h = halves[c][piece]
                    pieces[slot, at] = jnp.concatenate([-h, -h, h, h], 1)
                    at += 1

    def one_group(turn, do_scatter, do_gather):
        before = Codes(geo, codes, group_rows(turn - 1)) if do_scatter else None
        code = Codes(geo, codes, group_rows(turn)) if do_gather else None
        waiting = []
        ahead = AHEAD if do_gather and do_scatter else 0
        for t in range(GROUP + ahead):
            if do_gather and t >= ahead:
                one = t - ahead
                parts, level = gather_tile(turn, one, code.depth4), 0
                while (one >> level) & 1:
                    parts = [merged(x, y, level) for x, y in zip(waiting.pop(), parts)]
                    level += 1
                waiting.append(parts)
            if do_scatter and t < GROUP:
                scatter_tile(turn - 1, t, before.depth4, (turn - 1) & 1)
        if do_gather:
            pair_forces(turn, code, waiting.pop(), turn & 1)

    def looped(turn, carry):
        one_group(turn, True, True)
        return carry

    count = geo.tiles // GROUP
    fetch.wait()
    one_group(0, False, True)
    lax.fori_loop(1, count, looped, 0)
    one_group(count, True, False)

    gates = gates.astype(BF16)

    def folded(group):
        for c in range(3):
            for k in range(geo.bz + 1):
                parts = []
                for plane in range(planes):
                    rows = jnp.zeros((8, WINDOW), F32)
                    at = geo.bz * plane + k
                    if k < geo.bz:
                        rows = rows + sums[group, at, 16 * c : 16 * c + 8, :]
                    if k > 0:
                        rows = rows + sums[group, at - 1, 16 * c + 8 : 16 * c + 16, :]
                    parts.append(rows)
                rows = slice(ZR * c + 8 * k, ZR * c + 8 * k + 8)
                for pair in range(0, planes, 2):
                    lanes[pair // 2, rows, :] = jnp.concatenate(parts[pair : pair + 2], 1)
        joined = jnp.concatenate([lanes[pair] for pair in range(planes // 2)], 1)
        value = jnp.zeros((3 * ZR, LP), F32)
        for piece in split(joined):
            value = value + lax.dot_general(
                piece.astype(BF16), gates, (((1,), (1,)), ((), ())), preferred_element_type=F32
            )
        return value.reshape(3, ZR, LP)

    if both:
        frozen[...] = folded(1)
    force[...] = folded(0) + frozen[...]


def window_gates(geo):
    shape = (geo.LP, WINDOW * geo.bx * geo.by)
    lane = lax.broadcasted_iota(jnp.int32, shape, 0)
    column = lax.broadcasted_iota(jnp.int32, shape, 1)
    plane, cell = column // WINDOW, column % WINDOW
    x = 4 * (plane // geo.by) - 1 + cell // 8
    y = 4 * (plane % geo.by) - 1 + cell % 8
    inside = (x >= 0) & (x < geo.X) & (y >= 0) & (y < geo.Y)
    return jnp.where(inside & (lane == x * geo.Y + y), 1.0, 0.0)


def start_fetch(base, work):
    pltpu.make_async_copy(base, work[4], work[5]).start()


def first_kernel(
    geo, bases, face, rows_in, from_low, from_high, hots, codes, groups,
    u, u_old, jinv, frozen, force, zbuf, wide, *work,
):
    start_fetch(bases, work)
    targets = [u.at[c] for c in range(3)] + [u_old.at[c] for c in range(3)]
    targets = targets + [jinv.at[c] for c in range(9)]
    fill_done(geo, edges(), face, rows_in, from_low, from_high, wide, targets)
    pair_pass(geo, bases, u, hots, codes, groups, True, work, frozen, force)
    z_slab(geo, force, zbuf)


def next_kernel(
    geo, bases, face, rows_in, from_low, from_high, u, u_old, jinv, frozen, hots, codes, groups,
    new_u, norm, force, zbuf, wide, total, *work,
):
    start_fetch(bases, work)
    sum_done(geo, edges(), face, rows_in, from_low, from_high, wide, total)
    update(geo, total, u, u_old, jinv, new_u, norm)
    pair_pass(geo, bases, new_u, hots, codes, groups, False, work, frozen, force)
    z_slab(geo, force, zbuf)


def last_kernel(
    geo, face, rows_in, from_low, from_high, u, u_old, jinv, norm_0, norm_1,
    out, norms, wide, total, new_u, norm_2,
):
    sum_done(geo, edges(), face, rows_in, from_low, from_high, wide, total)
    update(geo, total, u, u_old, jinv, new_u, norm_2)
    for c in range(3):
        wide[...] = new_u[c, 2 : 2 + geo.sz, :].T
        for x in range(geo.sx):
            start = (x + 1) * geo.Y + 1
            out[c, x * geo.sy : (x + 1) * geo.sy, :] = wide[start : start + geo.sy, :]
    lane = lax.broadcasted_iota(jnp.int32, (1, geo.LP), 1)
    line = jnp.zeros((1, geo.LP), F32)
    for k, norm in enumerate((norm_0, norm_1, norm_2)):
        line = line + jnp.where(lane == k, jnp.sum(norm[...]), 0.0)
    norms[...] = jnp.broadcast_to(line, norms.shape)


def ring(shard, axis, by):
    count = lax.axis_size(axis)
    return lax.ppermute(shard, axis, [(i, (i + by) % count) for i in range(count)])


def swap(low_buffer, high_buffer, axis):
    return ring(high_buffer, axis, 1), ring(low_buffer, axis, -1)


def swap_joint(buffer, axis):
    if lax.axis_size(axis) <= 2:
        other = ring(buffer, axis, 1)
        return other, other
    return ring(buffer, axis, 1), ring(buffer, axis, -1)


def per_device(u_old, u_trial, jacobian_inverse, tile_base, pair_codes, pair_groups):
    sx, sy, sz = u_old.shape[1:]
    geo = Geo(sx, sy, sz, tile_base.shape[0])
    if sz != 128 or geo.LP != 128 or sy % 8 or geo.bx % 2 or geo.tiles % GROUP:
        raise ValueError("unsupported sizes")
    axes = ("gx", "gy", "gz")
    cells = 3.0 * sx * sy * sz
    devices = 1
    for axis in axes:
        devices = devices * lax.axis_size(axis)
    cells = cells * devices
    vmem, anywhere = pl.BlockSpec(memory_space=pltpu.VMEM), pl.BlockSpec(memory_space=pl.ANY)

    def arr(*shape):
        return jax.ShapeDtypeStruct(shape, F32)

    def call(kernel, name, bases, operands, outs, scratch=(), cost=None, flags=None):
        return pl.pallas_call(
            functools.partial(kernel, geo),
            out_shape=outs,
            in_specs=[anywhere] * len(bases) + [vmem] * len(operands),
            out_specs=[vmem] * len(outs),
            scratch_shapes=list(scratch),
            compiler_params=pltpu.CompilerParams(vmem_limit_bytes=VMEM_GRANT, flags=flags),
            cost_estimate=cost,
            name=name,
        )(*bases, *operands)

    def spot(*shape, dtype=F32):
        return pltpu.VMEM(shape, dtype)

    anchors = geo.bx * geo.by * geo.bz

    def work(count):
        return [
            spot(anchors, 48, 2 * WINDOW, dtype=BF16),
            spot(2, 6 * count, GROUP, 512),
            spot(count, anchors, 48, WINDOW),
            spot(max(2, geo.bx * geo.by // 2), 3 * geo.ZR, geo.LP),
            pltpu.SMEM((geo.tiles,), jnp.int32),
            pltpu.SemaphoreType.DMA(()),
        ]

    square = spot(geo.LP, sz)
    lattice = arr(3, geo.ZR, geo.LP)
    faces3, rows8, zshape = arr(3, geo.RP, sz), arr(8, geo.LP), arr(3, 8, geo.LP)
    slab = arr(3, geo.slab, 128)

    ut = u_trial.reshape(3, sx * sy, sz)
    uo = u_old.reshape(3, sx * sy, sz)
    ji = jacobian_inverse.reshape(9, sx * sy, sz)

    hots = call(
        hot_kernel,
        "hots",
        [],
        [pair_codes],
        [jax.ShapeDtypeStruct((geo.tiles, WINDOW, 512), BF16)],
        cost=pl.CostEstimate(flops=0, bytes_accessed=16 << 20, transcendentals=0),
    )[0]
    part_x = arr(15 * sy, 128)
    face, zbuf, x_low, x_high = call(
        fill_z_kernel,
        "fill_z",
        [],
        [jnp.concatenate([ut, uo, ji], 0)],
        [arr(15, geo.RP, sz), arr(32, geo.LP), part_x, part_x],
        [square],
    )
    z_low, z_high = swap_joint(zbuf, "gz")
    wide_x = arr(15 * sy + 32, 128)
    x_low, x_high = call(
        fill_x_kernel, "fill_x", [], [x_low, x_high, z_low, z_high], [wide_x, wide_x]
    )
    from_low, from_high = swap(x_low, x_high, "gx")
    wide_y = arr(fill_y_rows(geo), 128)
    face, rows, y_low, y_high = call(
        fill_y_kernel,
        "fill_y",
        [],
        [face, z_low, z_high, from_low, from_high],
        [arr(15, geo.RP, sz), arr(32, geo.LP), wide_y, wide_y],
    )
    from_low, from_high = swap(y_low, y_high, "gy")
    u, uo_l, ji_l, frozen, force, zbuf = call(
        first_kernel,
        "first_pass",
        [tile_base],
        [face, rows, from_low, from_high, hots, pair_codes, pair_groups],
        [lattice, lattice, arr(9, geo.ZR, geo.LP), lattice, lattice, zshape],
        [square] + work(2),
    )

    norm_list = []
    for iteration in range(ITERS):
        z_low, z_high = swap_joint(zbuf, "gz")
        face, rows, x_low, x_high = call(
            sum_x_kernel, "sum_x", [], [force, z_low, z_high], [faces3, rows8, slab, slab]
        )
        from_low, from_high = swap(x_low, x_high, "gx")
        face, rows, y_low, y_high = call(
            sum_y_kernel,
            "sum_y",
            [],
            [face, rows, from_low, from_high],
            [faces3, rows8, slab, slab],
        )
        from_low, from_high = swap(y_low, y_high, "gy")
        total = spot(3, geo.ZR, geo.LP)
        if iteration < ITERS - 1:
            u, norm, force, zbuf = call(
                next_kernel,
                "next_pass",
                [tile_base],
                [face, rows, from_low, from_high, u, uo_l, ji_l, frozen, hots, pair_codes, pair_groups],
                [lattice, rows8, lattice, zshape],
                [square, total] + work(1),
            )
            norm_list.append(norm)
    out, norms = call(
        last_kernel,
        "last",
        [],
        [face, rows, from_low, from_high, u, uo_l, ji_l] + norm_list,
        [arr(3, sx * sy, sz), arr(devices, 128)],
        [square, spot(3, geo.ZR, geo.LP), spot(3, geo.ZR, geo.LP), spot(8, geo.LP)],
    )
    spread = lax.all_to_all(norms.reshape(devices, 1, 128), axes, 0, 0)
    squares = jnp.sum(spread, axis=(0, 1))[:ITERS]
    return out.reshape(3, sx, sy, sz), jnp.sqrt(squares / cells)


def solution(mesh):
    return jax.shard_map(
        per_device,
        mesh=mesh,
        in_specs=(
            P(None, "gx", "gy", "gz"),
            P(None, "gx", "gy", "gz"),
            P(None, None, "gx", "gy", "gz"),
            P(("gx", "gy", "gz")),
            P(None, ("gx", "gy", "gz"), None),
            P(("gx", "gy", "gz"), None),
        ),
        out_specs=(P(None, "gx", "gy", "gz"), P()),
        check_vma=False,
    )
```
